32 devices in a mesh: sec: 8 (over y, x, core), img: 4 (over z).
Axes of the slice: x: 2, y: 2, z: 4, core: 2. Of those that a mesh axis runs over, the one named last changes fastest.
Arguments:
- saved_last: bfloat16 [8, 4, 4, 21, 21, 384], P('sec', None, 'img'), may hold values from -6 to 6
- saved_older: bfloat16 [8, 4, 4, 21, 21, 384], P('sec', None, 'img'), may hold values from -6 to 6
- arriving: bfloat16 [8, 2, 4, 21, 21, 384], P('sec', None, 'img'), may hold values from -6 to 6
- head_adjoint: bfloat16 [3, 2, 4, 21, 21, 384], P(None, None, 'img'), may hold values from -6 to 6
- plan: int32 [8, 4], P('sec'), may hold values from 0 to 3, each once within a row
- depth_five: bfloat16 [8, 25, 384], P('sec'), may hold values from -1.25 to 1.25
- depth_three: bfloat16 [8, 9, 384], P('sec'), may hold values from -2 to 2
- point_five: bfloat16 [8, 384, 384], P('sec'), may hold values from -0.3125 to 0.3125
- point_three: bfloat16 [8, 384, 384], P('sec'), may hold values from -0.3125 to 0.3125
Outputs:
- outgoing: bfloat16 [8, 2, 4, 21, 21, 384], P('sec', None, 'img')
- grad_point_five: float32 [8, 384, 384], P('sec', 'img')
- grad_depth_five: float32 [8, 384, 25], P('sec', 'img')
- grad_point_three: float32 [8, 384, 384], P('sec', 'img')
- grad_depth_three: float32 [8, 384, 9], P('sec', 'img')
The draws below stay inside these ranges and needn't reach their ends.
Inputs may be any that keep to these rules, and one draw needn't show every extreme that they name: `plan`: each row is a permutation of the stash slots.
All inputs are finite; a program needn't handle non-finite values.
Results may differ from the reference program's by a relative error of at most 0.012.
Values may be sent and summed in bfloat16 or wider, within the bound.
A program may use at most 128 MiB of HBM per device.

```python
import jax
import jax.numpy as jnp
from jax import lax

C = 384
HGT = 21
WID = 21
KFIVE = 5
KTHREE = 3
STEPS = 4
IMAGES = 4
CELLS = 8


def block_scale(own_key, dims, pieces, low, high):
    level, own = 1.0, jax.random.fold_in(own_key, 6)
    for dim, blocks in pieces:
        steps = jnp.exp(jax.random.uniform(jax.random.fold_in(own, dim), (blocks,), jnp.float32, low / len(pieces), high / len(pieces)))
        level = level * jnp.repeat(steps, dims[dim] // blocks).reshape([-1 if axis == dim else 1 for axis in range(len(dims))])
    return level


def bell_draw(rng, shape, scale, reach, split=(), dtype=jnp.bfloat16):
    drawn = scale * jax.random.normal(rng, shape, jnp.float32)
    if split:
        drawn = drawn * block_scale(rng, shape, split, -0.22, 0.18)
    return jnp.clip(drawn, -reach, reach).astype(dtype)


def setup_inputs(seed: int = 0) -> dict:
    keys = jax.random.split(jax.random.key(seed), 10)
    return {
        "saved_last": bell_draw(keys[0], (CELLS, STEPS, IMAGES, HGT, WID, C), 1.0, 6.0, ((0, 8), (2, 4))),
        "saved_older": bell_draw(keys[1], (CELLS, STEPS, IMAGES, HGT, WID, C), 1.0, 6.0, ((0, 8), (2, 4))),
        "arriving": bell_draw(keys[2], (CELLS, 2, IMAGES, HGT, WID, C), 1.0, 6.0, ((0, 8), (2, 4))),
        "head_adjoint": bell_draw(keys[3], (STEPS - 1, 2, IMAGES, HGT, WID, C), 1.0, 6.0, ((2, 4),)),
        "plan": jax.vmap(lambda own: jax.random.permutation(own, STEPS))(jax.random.split(keys[4], CELLS)).reshape((CELLS, STEPS)).astype(jnp.int32),
        "depth_five": bell_draw(keys[5], (CELLS, KFIVE * KFIVE, C), (KFIVE * KFIVE) ** -0.5, 1.25, ((0, 8),)),
        "depth_three": bell_draw(keys[6], (CELLS, KTHREE * KTHREE, C), (KTHREE * KTHREE) ** -0.5, 2.0, ((0, 8),)),
        "point_five": bell_draw(keys[7], (CELLS, C, C), C ** -0.5, 0.3125, ((0, 8),)),
        "point_three": bell_draw(keys[8], (CELLS, C, C), C ** -0.5, 0.3125, ((0, 8),)),
    }


def depth_apply(active, taps, kernel):
    radius = kernel // 2
    height, breadth = active.shape[1], active.shape[2]
    padded = jnp.pad(active, ((0, 0), (radius, radius), (radius, radius), (0, 0)))
    summed = jnp.zeros(active.shape, jnp.float32)
    for row_tap in range(kernel):
        for col_tap in range(kernel):
            window = padded[:, row_tap:row_tap + height, col_tap:col_tap + breadth, :].astype(jnp.float32)
            summed = summed + taps[row_tap * kernel + col_tap].astype(jnp.float32) * window
    return summed


def depth_transpose(back, taps, kernel):
    radius = kernel // 2
    height, breadth = back.shape[1], back.shape[2]
    padded = jnp.pad(back, ((0, 0), (radius, radius), (radius, radius), (0, 0)))
    summed = jnp.zeros(back.shape, jnp.float32)
    for row_tap in range(kernel):
        for col_tap in range(kernel):
            first_row = 2 * radius - row_tap
            first_col = 2 * radius - col_tap
            window = padded[:, first_row:first_row + height, first_col:first_col + breadth, :]
            summed = summed + taps[row_tap * kernel + col_tap].astype(jnp.float32) * window
    return summed


def depth_taps(active, back, kernel):
    radius = kernel // 2
    height, breadth = active.shape[1], active.shape[2]
    padded = jnp.pad(active, ((0, 0), (radius, radius), (radius, radius), (0, 0)))
    columns = []
    for row_tap in range(kernel):
        for col_tap in range(kernel):
            window = padded[:, row_tap:row_tap + height, col_tap:col_tap + breadth, :].astype(jnp.float32)
            columns.append(jnp.sum(window * back, axis=(0, 1, 2)))
    return jnp.stack(columns, 0)


def cell_backward(last_in, older_in, grad_out, grad_pass, taps_five, taps_three, weight_five, weight_three):
    channels = last_in.shape[3]
    pixels = last_in.shape[0] * last_in.shape[1] * last_in.shape[2]
    factor = 1.0 / (last_in.shape[1] * last_in.shape[2])
    active_last = jax.nn.relu(last_in)
    active_older = jax.nn.relu(older_in)
    mixed_five = depth_apply(active_last, taps_five, 5).astype(jnp.bfloat16)
    mixed_three = depth_apply(active_older, taps_three, 3).astype(jnp.bfloat16)
    flat_grad = grad_out.reshape(pixels, channels)
    back_five = jnp.dot(flat_grad, weight_five.T, preferred_element_type=jnp.float32).reshape(last_in.shape)
    back_three = jnp.dot(flat_grad, weight_three.T, preferred_element_type=jnp.float32).reshape(last_in.shape)
    through_five = depth_transpose(back_five, taps_five, 5)
    grad_last = (grad_pass.astype(jnp.float32) + grad_out.astype(jnp.float32)
                 + jnp.where(last_in > 0, through_five, 0.0)).astype(jnp.bfloat16)
    grad_older = jnp.where(older_in > 0, depth_transpose(back_three, taps_three, 3), 0.0).astype(jnp.bfloat16)
    point_grad_five = jnp.dot(mixed_five.reshape(pixels, channels).T, flat_grad, preferred_element_type=jnp.float32)
    point_grad_three = jnp.dot(mixed_three.reshape(pixels, channels).T, flat_grad, preferred_element_type=jnp.float32)
    taps_grad_five = depth_taps(active_last, back_five, 5)
    taps_grad_three = depth_taps(active_older, back_three, 3)
    grads_five = jnp.concatenate([point_grad_five, taps_grad_five.T], 1) * factor
    grads_three = jnp.concatenate([point_grad_three, taps_grad_three.T], 1) * factor
    return grad_last, grad_older, grads_five, grads_three


def reference(saved_last, saved_older, arriving, head_adjoint, plan, depth_five, depth_three, point_five, point_three):
    sections = saved_last.shape[0]
    turns = saved_last.shape[1]
    channels = saved_last.shape[5]
    totals_five = jnp.zeros((sections, channels, channels + 25), jnp.float32)
    totals_three = jnp.zeros((sections, channels, channels + 9), jnp.float32)
    pairs = arriving
    for turn_index in range(turns):
        if turn_index > 0:
            pairs = jnp.concatenate([pairs[1:], head_adjoint[turn_index - 1][None]], 0)

        def one_section(inputs):
            stash_last, stash_older, slot_index, adjoint_pair, taps_five, taps_three, weight_five, weight_three = inputs
            last_in = lax.dynamic_index_in_dim(stash_last, slot_index, 0, keepdims=False)
            older_in = lax.dynamic_index_in_dim(stash_older, slot_index, 0, keepdims=False)
            grad_last, grad_older, grads_five, grads_three = cell_backward(
                last_in, older_in, adjoint_pair[0], adjoint_pair[1], taps_five, taps_three, weight_five, weight_three)
            return jnp.stack([grad_last, grad_older], 0), grads_five, grads_three

        pairs, grads_five, grads_three = lax.map(one_section, (
            saved_last, saved_older, plan[:, turn_index], pairs, depth_five, depth_three, point_five, point_three))
        totals_five = totals_five + grads_five
        totals_three = totals_three + grads_three
    return (pairs, totals_five[:, :, :channels], totals_five[:, :, channels:],
            totals_three[:, :, :channels], totals_three[:, :, channels:])
```

```python
import functools

import jax
import jax.numpy as jnp
from jax import lax
from jax.experimental import pallas as pl
from jax.experimental.pallas import tpu as pltpu
from jax.sharding import PartitionSpec as P

F32 = jnp.float32
BF16 = jnp.bfloat16
LANES = 128
WIDE = 256
MESH = pl.DeviceIdType.MESH
CHUNKS = 3
GRANT = 36 * 2**20


def up(value, unit):
    return -(-value // unit) * unit


def turned(block, shift):
    shift = shift % block.shape[0]
    return block if shift == 0 else pltpu.roll(block, shift, 0)


def rows_at(even, odd, pair, offset, lanes):
    if offset % 2 == 0:
        block = even[pair + offset // 2 + 1, :, lanes]
    else:
        block = odd[pair + (offset + 1) // 2, :, lanes]
    return block.reshape(-1, 8, WIDE)


def filtered(even, odd, taps, kernel, pair, lanes, back):
    radius = kernel // 2
    held = [rows_at(even, odd, pair, k - radius, lanes) for k in range(kernel)]
    total = None
    for col_tap in range(kernel):
        part = None
        for row_tap in range(kernel):
            at = kernel - 1 - row_tap if back else row_tap
            term = taps[row_tap * kernel + col_tap, :, lanes][None] * held[at]
            part = term if part is None else part + term
        wide = part.astype(F32).reshape(-1, WIDE)
        moved = turned(wide, col_tap - radius if back else radius - col_tap)
        total = moved if total is None else total + moved
    return total


def tap_sums(even, odd, back, sums, kernel, pair, lanes):
    radius = kernel // 2
    held = [rows_at(even, odd, pair, k - radius, lanes) for k in range(kernel)]
    wide = back[pair + 1, :, lanes].astype(F32)
    for col_tap in range(kernel):
        moved = turned(wide, col_tap - radius).astype(BF16).reshape(-1, 8, WIDE)
        for row_tap in range(kernel):
            term = held[row_tap] * moved
            folded = term[0]
            for part in range(1, term.shape[0]):
                folded = folded + term[part]
            tap = row_tap * kernel + col_tap
            sums[tap, :, lanes] = sums[tap, :, lanes] + folded.astype(F32)


def kernel_body(
    sections,
    group,
    kernels,
    spans,
    plan,
    last,
    older,
    arriving,
    head,
    depth_five,
    depth_three,
    point_five,
    point_three,
    outgoing,
    out_five,
    out_three,
    out_taps_five,
    out_taps_three,
    inbox,
    outbox,
    final,
    stage,
    even_last,
    odd_last,
    even_older,
    odd_older,
    even_five,
    odd_five,
    even_three,
    odd_three,
    mixed_five,
    mixed_three,
    taps_five,
    taps_three,
    total_five,
    total_three,
    sums_five,
    sums_three,
    sums_all,
    give_five,
    give_three,
    give_taps,
    take_five,
    take_three,
    take_taps,
    local_sem,
    send_sem,
    recv_sem,
    give_sem,
    take_sem,
    final_sem,
):
    five, three = kernels
    turns, height, width, channels = last.shape
    breadth = stage.shape[1]
    rows = channels // group
    factor = 1.0 / (height * width)
    blocks = 2 * channels // WIDE
    columns = channels // LANES
    pairs = spans[-1][1]
    end = turns - 1
    sec = lax.axis_index("sec")
    img = lax.axis_index("img")
    top = sec == sections - 1
    bottom = sec == 0
    not_top = sec < sections - 1
    not_bottom = sec > 0

    def lines(span):
        return 2 * span[0], min(2 * span[1], height)

    def first_copy(which):
        target = inbox.at[0, which, pl.ds(0, height)]
        return pltpu.make_async_copy(arriving.at[which], target, local_sem.at[0, which])

    def head_copy(turn, which):
        source = head.at[turn - 1, which]
        target = inbox.at[turn, which, pl.ds(0, height)]
        return pltpu.make_async_copy(source, target, local_sem.at[turn, which])

    for which in range(2):
        first_copy(which).start()

    @pl.when(top)
    def _():
        for turn in range(1, turns):
            for which in range(2):
                head_copy(turn, which).start()

    barrier = pltpu.get_barrier_semaphore()
    for step in range(1, group):
        pl.semaphore_signal(
            barrier,
            inc=1,
            device_id={"sec": sec, "img": lax.rem(img + step, group)},
            device_id_type=MESH,
        )

    @pl.when(not_bottom)
    def _():
        pl.semaphore_signal(
            barrier, inc=1, device_id={"sec": sec - 1, "img": img}, device_id_type=MESH
        )

    @pl.when(not_top)
    def _():
        pl.semaphore_signal(
            barrier, inc=1, device_id={"sec": sec + 1, "img": img}, device_id_type=MESH
        )

    edge_even = jnp.zeros(even_five.shape[2:], BF16)

    def clear(turn, carry):
        for ref in (even_last, even_older, even_five, even_three):
            ref[turn, 0] = edge_even
            ref[turn, pairs + 1] = edge_even
        for ref in (odd_last, odd_older, odd_five, odd_three):
            ref[turn, pairs] = edge_even
        return carry

    lax.fori_loop(0, turns, clear, 0)
    for row in range(stage.shape[0]):
        stage[row, breadth - 8 : breadth] = jnp.zeros((8, channels), F32)
    for row in (0, *range(height + 1, stage.shape[0])):
        stage[row] = jnp.zeros((breadth, channels), F32)
    for wide, packed in ((depth_five, taps_five), (depth_three, taps_three)):
        for tap in range(packed.shape[0]):
            value = jnp.broadcast_to(wide[tap : tap + 1].astype(F32), (8, channels))
            packed[tap] = jnp.concatenate([value, value], 1).astype(BF16)

    def prepare(turn):
        slot = plan[0, turn]
        for saved, even, odd in ((last, even_last, odd_last), (older, even_older, odd_older)):

            def one(row, carry):
                stage[row + 1, 0:width, :] = jnp.maximum(saved[slot, row].astype(F32), 0.0)
                return carry

            lax.fori_loop(0, height, one, 0, unroll=3)

            def two(pair, carry):
                rows = [stage[2 * pair + k] for k in range(3)]
                odd[turn, pair] = jnp.concatenate(rows[0:2], 1).astype(BF16)
                even[turn, pair + 1] = jnp.concatenate(rows[1:3], 1).astype(BF16)
                return carry

            lax.fori_loop(0, pairs, two, 0)

    def hop(turn, which, part):
        start, stop = lines(spans[part])
        return pltpu.make_async_remote_copy(
            src_ref=outbox.at[turn, which, pl.ds(start, stop - start)],
            dst_ref=inbox.at[turn + 1, which, pl.ds(start, stop - start)],
            send_sem=send_sem.at[turn, which, part],
            recv_sem=recv_sem.at[turn, which, part],
            device_id={"sec": lax.max(sec - 1, 0), "img": img},
            device_id_type=MESH,
        )

    def arrive(turn, which, part):
        if part == 0:

            @pl.when(jnp.logical_and(turn > 0, top))
            def _():
                head_copy(turn, which).wait()

        @pl.when(jnp.logical_and(turn > 0, not_top))
        def _():
            hop(turn - 1, which, part).wait_recv()

    def pull(turn, part):
        start, stop = lines(spans[part])
        grad = inbox[turn, 0, start:stop].reshape(-1, channels)
        for weights, even, odd in (
            (point_five, even_five, odd_five),
            (point_three, even_three, odd_three),
        ):
            product = lax.dot_general(
                grad, weights[...], (((1,), (1,)), ((), ())), preferred_element_type=F32
            )

            def line(row):
                if start <= row < stop:
                    at = (row - start) * breadth
                    return product[at : at + breadth].astype(BF16)
                if 0 < row < start:
                    return even[turn, row // 2 + 1, :, (row % 2) * channels : (row % 2 + 1) * channels]
                return jnp.zeros((breadth, channels), BF16)

            for pair in range(*spans[part]):
                for side in range(2):
                    lanes = slice(side * channels, (side + 1) * channels)
                    even[turn, pair + 1, :, lanes] = line(2 * pair + side)
                    odd[turn, pair, :, lanes] = line(2 * pair - 1 + side)

    def parts(pair, block):
        for part in range(WIDE // LANES):
            at = block * (WIDE // LANES) + part
            lanes = slice((at % columns) * LANES, (at % columns + 1) * LANES)
            yield 2 * pair + at // columns, lanes, slice(part * LANES, (part + 1) * LANES)

    def each_block(work, span):
        def one(pair, carry):
            for block in range(blocks):
                work(pair, block, slice(block * WIDE, (block + 1) * WIDE))
            return carry

        lax.fori_loop(span[0], span[1], one, 0)

    def through_five(turn, target, span):
        wide_to = target.shape[1]

        def work(pair, block, wide):
            out = filtered(
                even_five.at[turn], odd_five.at[turn], taps_five, five, pair, wide, True
            )
            kept = jnp.where(even_last[turn, pair + 1, :, wide].astype(F32) > 0, out, 0.0)
            for at, lanes, cut in parts(pair, block):
                own = inbox[turn, 0, at, :, lanes].astype(F32)
                extra = inbox[turn, 1, at, :, lanes].astype(F32)
                done = kept[:, cut] + own + extra
                target[at, :, lanes] = done[0:wide_to].astype(BF16)

        each_block(work, span)

    def through_three(turn, target, span):
        wide_to = target.shape[1]

        def work(pair, block, wide):
            out = filtered(
                even_three.at[turn], odd_three.at[turn], taps_three, three, pair, wide, True
            )
            kept = jnp.where(even_older[turn, pair + 1, :, wide].astype(F32) > 0, out, 0.0)
            for at, lanes, cut in parts(pair, block):
                target[at, :, lanes] = kept[0:wide_to, cut].astype(BF16)

        each_block(work, span)

    def forward(turn, span):
        def work(pair, block, wide):
            for even, odd, taps, mixed, kernel in (
                (even_last, odd_last, taps_five, mixed_five, five),
                (even_older, odd_older, taps_three, mixed_three, three),
            ):
                out = filtered(even.at[turn], odd.at[turn], taps, kernel, pair, wide, False)
                for at, lanes, cut in parts(pair, block):
                    mixed[at, :, lanes] = out[:, cut].astype(BF16)

        each_block(work, span)

    def add_taps(turn):
        def work(pair, block, wide):
            tap_sums(
                even_last.at[turn], odd_last.at[turn], even_five.at[turn], sums_five, five, pair, wide
            )
            tap_sums(
                even_older.at[turn], odd_older.at[turn], even_three.at[turn], sums_three, three, pair, wide
            )

        each_block(work, (0, pairs))

    def add_point(turn, mixed, total):
        flat = mixed[0:height].reshape(-1, channels)
        grad = inbox[turn, 0, 0:height].reshape(-1, channels)
        total[...] += lax.dot_general(
            flat, grad, (((0,), (0,)), ((), ())), preferred_element_type=F32
        )

    def share(part, step):
        source = (give_three, give_five, give_taps)[part]
        target = (take_three, take_five, take_taps)[part]
        peer = lax.rem(img + step, group)
        return pltpu.make_async_remote_copy(
            src_ref=source.at[peer],
            dst_ref=target.at[step],
            send_sem=give_sem.at[part, step],
            recv_sem=take_sem.at[part, step],
            device_id={"sec": sec, "img": peer},
            device_id_type=MESH,
        )

    prepare(0)
    callers = group + 1 - bottom.astype(jnp.int32) - top.astype(jnp.int32)
    pl.semaphore_wait(barrier, callers)
    for ref in (sums_five, sums_three, total_five, total_three, sums_all):
        ref[...] = jnp.zeros(ref.shape, ref.dtype)
    first_copy(0).wait()
    first_copy(1).wait()

    def turn_work(turn, carry):
        def ready(part):
            arrive(turn, 1, part)
            for which, through in ((0, through_five), (1, through_three)):
                through(turn, outbox.at[turn, which], spans[part])

                @pl.when(not_bottom)
                def _():
                    hop(turn, which, part).start()

        for part in range(len(spans)):
            arrive(turn, 0, part)
            pull(turn, part)
            if part > 0:
                ready(part - 1)
            if part + 1 < len(spans):
                forward(turn, spans[part])
        ready(len(spans) - 1)
        forward(turn, spans[-1])
        add_point(turn, mixed_five, total_five)
        add_point(turn, mixed_three, total_three)
        prepare(turn + 1)
        return carry

    lax.fori_loop(0, end, turn_work, 0)

    forward(end, (0, pairs))
    for part in range(len(spans)):
        arrive(end, 0, part)
    for part, mixed, total, give in (
        (0, mixed_three, total_three, give_three),
        (1, mixed_five, total_five, give_five),
    ):
        add_point(end, mixed, total)
        for peer in range(group):
            give[peer] = (total[peer * rows : (peer + 1) * rows] * factor).astype(BF16)
        for step in range(1, group):
            share(part, step).start()
    for part in range(len(spans)):
        pull(end, part)

    def all_taps(turn, carry):
        add_taps(turn)
        return carry

    lax.fori_loop(0, turns, all_taps, 0)
    count_five, count_three = five * five, three * three
    for sums, start, count in ((sums_five, 0, count_five), (sums_three, count_five, count_three)):
        folded = jnp.sum(sums[...], axis=1)
        sums_all[start : start + count] = folded[:, 0:channels] + folded[:, channels:]
    flipped = sums_all[...].T * factor
    for peer in range(group):
        give_taps[peer] = flipped[peer * rows : (peer + 1) * rows].astype(BF16)
    for step in range(1, group):
        share(2, step).start()
    for part in range(len(spans)):
        arrive(end, 1, part)
    through_five(end, final.at[0], (0, pairs))
    through_three(end, final.at[1], (0, pairs))
    finals = [
        pltpu.make_async_copy(
            final.at[which, pl.ds(0, height)], outgoing.at[which], final_sem.at[which]
        )
        for which in range(2)
    ]
    for copy in finals:
        copy.start()

    def gathered(part, give, take):
        value = give[img].astype(F32)
        for step in range(1, group):
            share(part, step).wait_recv()
            value = value + take[step].astype(F32)
        return value

    out_three[...] = gathered(0, give_three, take_three)
    out_five[...] = gathered(1, give_five, take_five)
    by_tap = gathered(2, give_taps, take_taps).T
    for tap in range(count_five):
        out_taps_five[tap] = by_tap[tap : tap + 1]
    for tap in range(count_three):
        out_taps_three[tap] = by_tap[count_five + tap : count_five + tap + 1]
    for part in range(3):
        for step in range(1, group):
            share(part, step).wait_send()
    for copy in finals:
        copy.wait()

    @pl.when(not_bottom)
    def _():
        for turn in range(end):
            for which in range(2):
                for part in range(len(spans)):
                    hop(turn, which, part).wait_send()


def local(
    sections,
    group,
    saved_last,
    saved_older,
    arriving,
    head_adjoint,
    plan,
    depth_five,
    depth_three,
    point_five,
    point_three,
):
    turns, _, height, width, channels = saved_last.shape[1:]
    count_five, count_three = depth_five.shape[1], depth_three.shape[1]
    five, three = round(count_five**0.5), round(count_three**0.5)
    breadth = up(width + five // 2, 8)
    pairs = up(height, 2) // 2
    even = pltpu.VMEM((turns, pairs + 2, breadth, 2 * channels), BF16)
    odd = pltpu.VMEM((turns, pairs + 1, breadth, 2 * channels), BF16)
    rows = channels // group
    chunk = -(-pairs // CHUNKS)
    spans = tuple((at, min(at + chunk, pairs)) for at in range(0, pairs, chunk))
    vmem = pl.BlockSpec(memory_space=pltpu.VMEM)
    smem = pl.BlockSpec(memory_space=pltpu.SMEM)
    outside = pl.BlockSpec(memory_space=pl.ANY)
    body = functools.partial(kernel_body, sections, group, (five, three), spans)
    grow = (0, breadth - width)
    outgoing, grad_five, grad_three, taps_five, taps_three = pl.pallas_call(
        body,
        out_shape=(
            jax.ShapeDtypeStruct((2, height, width, channels), BF16),
            jax.ShapeDtypeStruct((rows, channels), F32),
            jax.ShapeDtypeStruct((rows, channels), F32),
            jax.ShapeDtypeStruct((count_five, 1, rows), F32),
            jax.ShapeDtypeStruct((count_three, 1, rows), F32),
        ),
        in_specs=[smem, vmem, vmem, *[outside] * 2, *[vmem] * 4],
        out_specs=(outside, *[vmem] * 4),
        scratch_shapes=[
            pltpu.VMEM((turns, 2, 2 * pairs, breadth, channels), BF16),
            pltpu.VMEM((turns - 1, 2, 2 * pairs, breadth, channels), BF16),
            pltpu.VMEM((2, 2 * pairs, width, channels), BF16),
            pltpu.VMEM((2 * pairs + 2, breadth, channels), F32),
            *([even, odd] * 4),
            pltpu.VMEM((2 * pairs, breadth, channels), BF16),
            pltpu.VMEM((2 * pairs, breadth, channels), BF16),
            pltpu.VMEM((count_five, 8, 2 * channels), BF16),
            pltpu.VMEM((count_three, 8, 2 * channels), BF16),
            pltpu.VMEM((channels, channels), F32),
            pltpu.VMEM((channels, channels), F32),
            pltpu.VMEM((count_five, 8, 2 * channels), F32),
            pltpu.VMEM((count_three, 8, 2 * channels), F32),
            pltpu.VMEM((LANES, channels), F32),
            pltpu.VMEM((group, rows, channels), BF16),
            pltpu.VMEM((group, rows, channels), BF16),
            pltpu.VMEM((group, rows, LANES), BF16),
            pltpu.VMEM((group, rows, channels), BF16),
            pltpu.VMEM((group, rows, channels), BF16),
            pltpu.VMEM((group, rows, LANES), BF16),
            pltpu.SemaphoreType.DMA((turns, 2)),
            pltpu.SemaphoreType.DMA((turns - 1, 2, len(spans))),
            pltpu.SemaphoreType.DMA((turns - 1, 2, len(spans))),
            pltpu.SemaphoreType.DMA((3, group)),
            pltpu.SemaphoreType.DMA((3, group)),
            pltpu.SemaphoreType.DMA((2,)),
        ],
        compiler_params=pltpu.CompilerParams(
            collective_id=0, has_side_effects=True, vmem_limit_bytes=GRANT
        ),
    )(
        plan,
        saved_last.reshape(turns, height, width, channels),
        saved_older.reshape(turns, height, width, channels),
        jnp.pad(arriving[0, :, 0], ((0, 0), (0, 0), grow, (0, 0))),
        jnp.pad(head_adjoint[:, :, 0], ((0, 0), (0, 0), (0, 0), grow, (0, 0))),
        depth_five[0],
        depth_three[0],
        point_five[0],
        point_three[0],
    )
    return (
        outgoing.reshape(1, 2, 1, height, width, channels),
        grad_five[None],
        taps_five.transpose(1, 2, 0),
        grad_three[None],
        taps_three.transpose(1, 2, 0),
    )


def solution(mesh):
    placed = (
        P("sec", None, "img", None, None, None),
        P("sec", None, "img", None, None, None),
        P("sec", None, "img", None, None, None),
        P(None, None, "img", None, None, None),
        P("sec", None),
        P("sec", None, None),
        P("sec", None, None),
        P("sec", None, None),
        P("sec", None, None),
    )
    return jax.shard_map(
        functools.partial(local, mesh.shape["sec"], mesh.shape["img"]),
        mesh=mesh,
        in_specs=placed,
        out_specs=(
            P("sec", None, "img", None, None, None),
            P("sec", "img", None),
            P("sec", "img", None),
            P("sec", "img", None),
            P("sec", "img", None),
        ),
        check_vma=False,
    )
```

```python
import functools

import jax
import jax.numpy as jnp
import numpy as np
from jax import lax
from jax.experimental import pallas as pl
from jax.experimental.pallas import tpu as pltpu
from jax.sharding import PartitionSpec as P

F32 = jnp.float32
BF16 = jnp.bfloat16
LANES = 128
WIDE = 256
MESH = pl.DeviceIdType.MESH
TWO = 2
CHUNKS = 3
GRANT = 36 * 2**20


def up(value, unit):
    return -(-value // unit) * unit


def turned(block, shift):
    shift = shift % block.shape[0]
    return block if shift == 0 else pltpu.roll(block, shift, 0)


def rows_at(even, odd, pair, offset, lanes):
    if offset % 2 == 0:
        block = even[pair + offset // 2 + 1, :, lanes]
    else:
        block = odd[pair + (offset + 1) // 2, :, lanes]
    return block.reshape(-1, 8, WIDE)


def rolled(even, odd, taps, kernel, pair, lanes, back):
    radius = kernel // 2
    held = [rows_at(even, odd, pair, k - radius, lanes) for k in range(kernel)]
    total = None
    for col_tap in range(kernel):
        part = None
        for row_tap in range(kernel):
            at = kernel - 1 - row_tap if back else row_tap
            term = taps[row_tap * kernel + col_tap, :, lanes][None] * held[at]
            part = term if part is None else part + term
        wide = part.astype(F32).reshape(-1, WIDE)
        moved = turned(wide, col_tap - radius if back else radius - col_tap)
        total = moved if total is None else total + moved
    return total


def filtered(even, odd, taps, kernel, group, select, parts, back):
    radius = kernel // 2
    breadth, wides = even.shape[1:]
    for slot, pair in enumerate(group):
        for first in range(0, wides, WIDE):
            lanes = slice(first, first + WIDE)
            held = [rows_at(even, odd, pair, k - radius, lanes) for k in range(kernel)]
            for col_tap in range(kernel):
                part = None
                for row_tap in range(kernel):
                    at = kernel - 1 - row_tap if back else row_tap
                    term = taps[row_tap * kernel + col_tap, :, lanes][None] * held[at]
                    part = term if part is None else part + term
                at = slot * LANES + col_tap * breadth
                parts[at : at + breadth, lanes] = part.reshape(breadth, WIDE)
    return lax.dot_general(
        select[...], parts[...], (((1,), (0,)), ((), ())), preferred_element_type=F32
    )


def selection(breadth, width, kernel, back):
    table = np.zeros((TWO * breadth, TWO * LANES), np.float32)
    for slot in range(TWO):
        for col_tap in range(kernel):
            shift = kernel // 2 - col_tap if back else col_tap - kernel // 2
            for col in range(width):
                if 0 <= col + shift < width:
                    at = slot * LANES + col_tap * breadth + col + shift
                    table[slot * breadth + col, at] = 1.0
    return jnp.asarray(table, BF16)


def tap_folds(even, odd, back, folds, kernel, pair):
    radius = kernel // 2
    breadth, wides = even.shape[1:]
    for first in range(0, wides, WIDE):
        lanes = slice(first, first + WIDE)
        held = [rows_at(even, odd, pair, k - radius, lanes) for k in range(kernel)]
        wide = back[pair + 1, :, lanes].astype(F32)
        for col_tap in range(kernel):
            other = turned(wide, col_tap - radius).astype(BF16).reshape(-1, 8, WIDE)
            for row_tap in range(kernel):
                term = held[row_tap] * other
                folded = term[0]
                for part in range(1, term.shape[0]):
                    folded = folded + term[part]
                tap = row_tap * kernel + col_tap
                folds[tap * 8 : tap * 8 + 8, lanes] = folded


def gathering(count):
    table = np.zeros((up(count, 8), up(count * 8, LANES)), np.float32)
    for tap in range(count):
        table[tap, tap * 8 : tap * 8 + 8] = 1.0
    return jnp.asarray(table, BF16)


def selection(breadth, width, kernel, back):
    table = np.zeros((TWO * breadth, TWO * LANES), np.float32)
    for slot in range(TWO):
        for col_tap in range(kernel):
            shift = kernel // 2 - col_tap if back else col_tap - kernel // 2
            for col in range(width):
                if 0 <= col + shift < width:
                    at = slot * LANES + col_tap * breadth + col + shift
                    table[slot * breadth + col, at] = 1.0
    return jnp.asarray(table, BF16)


def tap_sums(even, odd, back, sums, kernel, pair, lanes):
    radius = kernel // 2
    held = [rows_at(even, odd, pair, k - radius, lanes) for k in range(kernel)]
    wide = back[pair + 1, :, lanes].astype(F32)
    for col_tap in range(kernel):
        moved = turned(wide, col_tap - radius).astype(BF16).reshape(-1, 8, WIDE)
        for row_tap in range(kernel):
            term = held[row_tap] * moved
            folded = term[0]
            for part in range(1, term.shape[0]):
                folded = folded + term[part]
            tap = row_tap * kernel + col_tap
            sums[tap, :, lanes] = sums[tap, :, lanes] + folded.astype(F32)


def kernel_body(
    sections,
    group,
    kernels,
    spans,
    plan,
    last,
    older,
    arriving,
    head,
    depth_five,
    depth_three,
    point_five,
    point_three,
    select_five,
    select_three,
    select_five_back,
    select_three_back,
    gather_five,
    gather_three,
    outgoing,
    out_five,
    out_three,
    out_taps_five,
    out_taps_three,
    inbox,
    outbox,
    final,
    even_last,
    odd_last,
    even_older,
    odd_older,
    even_five,
    odd_five,
    even_three,
    odd_three,
    mixed_five,
    mixed_three,
    parts_five,
    parts_three,
    point_both,
    folds_five,
    folds_three,
    taps_five,
    taps_three,
    total_five,
    total_three,
    sums_five,
    sums_three,
    sums_all,
    give_five,
    give_three,
    give_taps,
    take_five,
    take_three,
    take_taps,
    relay_three,
    relay_five,
    local_sem,
    send_sem,
    recv_sem,
    give_sem,
    take_sem,
    final_sem,
):
    five, three = kernels
    turns, height, width, channels = last.shape
    breadth = inbox.shape[3]
    rows = channels // group
    factor = 1.0 / (height * width)
    pairs = spans[-1][1]
    blocks = 2 * channels // WIDE
    columns = channels // LANES
    end = turns - 1
    folded = group == 4
    sec = lax.axis_index("sec")
    img = lax.axis_index("img")
    top = sec == sections - 1
    bottom = sec == 0
    not_top = sec < sections - 1
    not_bottom = sec > 0

    def lines(span):
        return 2 * span[0], min(2 * span[1], height)

    def first_copy(which):
        target = inbox.at[0, which, pl.ds(0, height)]
        return pltpu.make_async_copy(arriving.at[which], target, local_sem.at[0, which])

    def head_copy(turn, which):
        source = head.at[turn - 1, which]
        target = inbox.at[turn, which, pl.ds(0, height)]
        return pltpu.make_async_copy(source, target, local_sem.at[turn, which])

    for which in range(2):
        first_copy(which).start()

    @pl.when(top)
    def _():
        for turn in range(1, turns):
            for which in range(2):
                head_copy(turn, which).start()

    barrier = pltpu.get_barrier_semaphore()
    for step in range(1, group):
        pl.semaphore_signal(
            barrier,
            inc=1,
            device_id={"sec": sec, "img": lax.rem(img + step, group)},
            device_id_type=MESH,
        )

    @pl.when(not_bottom)
    def _():
        pl.semaphore_signal(
            barrier, inc=1, device_id={"sec": sec - 1, "img": img}, device_id_type=MESH
        )

    @pl.when(not_top)
    def _():
        pl.semaphore_signal(
            barrier, inc=1, device_id={"sec": sec + 1, "img": img}, device_id_type=MESH
        )

    edge_even = jnp.zeros(even_five.shape[2:], BF16)

    def clear(turn, carry):
        for ref in (even_last, even_older, even_five, even_three):
            ref[turn, 0] = edge_even
            ref[turn, pairs + 1] = edge_even
        for ref in (odd_last, odd_older, odd_five, odd_three):
            ref[turn, pairs] = edge_even
        return carry

    lax.fori_loop(0, turns, clear, 0)
    for wide, packed in ((depth_five, taps_five), (depth_three, taps_three)):
        for tap in range(packed.shape[0]):
            value = jnp.broadcast_to(wide[tap : tap + 1].astype(F32), (8, channels))
            packed[tap] = jnp.concatenate([value, value], 1).astype(BF16)

    def prepare(turn):
        slot = plan[0, turn]
        zeros = jnp.zeros((breadth, channels), BF16)
        edge = jnp.zeros((breadth - width, channels), F32)
        for saved, even, odd in ((last, even_last, odd_last), (older, even_older, odd_older)):
            for row in range(-1, 2 * pairs):
                inside = 0 <= row < height
                active = zeros
                if inside:
                    raised = jnp.maximum(saved[slot, row], 0).astype(F32)
                    active = jnp.concatenate([raised, edge], 0).astype(BF16)
                lanes = slice((row % 2) * channels, (row % 2 + 1) * channels)
                if row >= 0:
                    even[turn, row // 2 + 1, :, lanes] = active
                if row < 2 * pairs - 1:
                    lanes = slice((1 - row % 2) * channels, (2 - row % 2) * channels)
                    odd[turn, (row + 1) // 2, :, lanes] = active

    def hop(turn, which, part):
        start, stop = lines(spans[part])
        return pltpu.make_async_remote_copy(
            src_ref=outbox.at[turn, which, pl.ds(start, stop - start)],
            dst_ref=inbox.at[turn + 1, which, pl.ds(start, stop - start)],
            send_sem=send_sem.at[turn, which, part],
            recv_sem=recv_sem.at[turn, which, part],
            device_id={"sec": lax.max(sec - 1, 0), "img": img},
            device_id_type=MESH,
        )

    def arrive(turn, which, part):
        if part == 0:

            @pl.when(jnp.logical_and(turn > 0, top))
            def _():
                head_copy(turn, which).wait()

        @pl.when(jnp.logical_and(turn > 0, not_top))
        def _():
            hop(turn - 1, which, part).wait_recv()

    def pull(turn):
        grad = inbox[turn, 0, 0:height].reshape(-1, channels)
        product = lax.dot_general(
            grad, point_both[...], (((1,), (1,)), ((), ())), preferred_element_type=F32
        )
        for even, odd, first in (
            (even_five, odd_five, 0),
            (even_three, odd_three, channels),
        ):

            def line(row):
                if 0 <= row < height:
                    at = row * breadth
                    return product[at : at + breadth, first : first + channels].astype(BF16)
                return jnp.zeros((breadth, channels), BF16)

            for pair in range(pairs):
                for side in range(2):
                    lanes = slice(side * channels, (side + 1) * channels)
                    even[turn, pair + 1, :, lanes] = line(2 * pair + side)
                    odd[turn, pair, :, lanes] = line(2 * pair - 1 + side)

    def parts(pair, block):
        for part in range(WIDE // LANES):
            at = block * (WIDE // LANES) + part
            lanes = slice((at % columns) * LANES, (at % columns + 1) * LANES)
            yield 2 * pair + at // columns, lanes, slice(part * LANES, (part + 1) * LANES)

    def each_block(work, span):
        def one(pair, carry):
            for block in range(blocks):
                work(pair, block, slice(block * WIDE, (block + 1) * WIDE))
            return carry

        lax.fori_loop(span[0], span[1], one, 0)

    def compact_five(turn, target, span):
        wide_to = target.shape[1]

        def work(pair, block, wide):
            out = rolled(
                even_five.at[turn], odd_five.at[turn], taps_five, five, pair, wide, True
            )
            kept = jnp.where(even_last[turn, pair + 1, :, wide].astype(F32) > 0, out, 0.0)
            for at, lanes, cut in parts(pair, block):
                own = inbox[turn, 0, at, :, lanes].astype(F32)
                extra = inbox[turn, 1, at, :, lanes].astype(F32)
                done = kept[:, cut] + own + extra
                target[at, :, lanes] = done[0:wide_to].astype(BF16)

        each_block(work, span)

    def compact_three(turn, target, span):
        wide_to = target.shape[1]

        def work(pair, block, wide):
            out = rolled(
                even_three.at[turn], odd_three.at[turn], taps_three, three, pair, wide, True
            )
            kept = jnp.where(even_older[turn, pair + 1, :, wide].astype(F32) > 0, out, 0.0)
            for at, lanes, cut in parts(pair, block):
                target[at, :, lanes] = kept[0:wide_to, cut].astype(BF16)

        each_block(work, span)

    def groups(span):
        for count, first in enumerate(range(span[0], span[1], TWO)):
            yield count % 2, range(first, min(first + TWO, span[1]))

    def sides(group, out):
        for slot, pair in enumerate(group):
            for side in range(2):
                lanes = slice(side * channels, (side + 1) * channels)
                at = slot * breadth
                yield pair, 2 * pair + side, lanes, out[at : at + breadth, lanes]

    def through_five(turn, target, span):
        wide_to = target.shape[1]
        for odds, group in groups(span):
            out = filtered(
                even_five.at[turn],
                odd_five.at[turn],
                taps_five,
                five,
                group,
                select_five_back,
                parts_five.at[odds],
                True,
            )
            for pair, row, lanes, value in sides(group, out):
                kept = jnp.where(even_last[turn, pair + 1, :, lanes].astype(F32) > 0, value, 0.0)
                own = inbox[turn, 0, row].astype(F32)
                extra = inbox[turn, 1, row].astype(F32)
                target[row] = (kept + own + extra)[0:wide_to].astype(BF16)

    def through_three(turn, target, span):
        wide_to = target.shape[1]
        for odds, group in groups(span):
            out = filtered(
                even_three.at[turn],
                odd_three.at[turn],
                taps_three,
                three,
                group,
                select_three_back,
                parts_three.at[odds],
                True,
            )
            for pair, row, lanes, value in sides(group, out):
                kept = jnp.where(even_older[turn, pair + 1, :, lanes].astype(F32) > 0, value, 0.0)
                target[row] = kept[0:wide_to].astype(BF16)

    def forward(turn, span):
        for odds, group in groups(span):
            for even, odd, taps, mixed, kernel, select, held in (
                (even_last, odd_last, taps_five, mixed_five, five, select_five, parts_five),
                (even_older, odd_older, taps_three, mixed_three, three, select_three, parts_three),
            ):
                out = filtered(
                    even.at[turn], odd.at[turn], taps, kernel, group, select, held.at[odds], False
                )
                for pair, row, lanes, value in sides(group, out):
                    mixed[lax.rem(turn, 2), row] = value.astype(BF16)

    def add_taps(turn):
        for pair in range(pairs):
            for even, odd, back, folds, gathers, sums, kernel in (
                (even_last, odd_last, even_five, folds_five, gather_five, sums_five, five),
                (even_older, odd_older, even_three, folds_three, gather_three, sums_three, three),
            ):
                held = folds.at[pair % 2]
                tap_folds(even.at[turn], odd.at[turn], back.at[turn], held, kernel, pair)
                sums[...] += jnp.dot(gathers[...], held[...], preferred_element_type=F32)

    def add_point(turn, mixed, total):
        flat = mixed[0:height].reshape(-1, channels)
        grad = inbox[turn, 0, 0:height].reshape(-1, channels)
        total[...] += lax.dot_general(
            flat, grad, (((0,), (0,)), ((), ())), preferred_element_type=F32
        )

    def share(part, step):
        source = (give_three, give_five, give_taps)[part]
        target = (take_three, take_five, take_taps)[part]
        peer = lax.rem(img + step, group)
        return pltpu.make_async_remote_copy(
            src_ref=source.at[peer],
            dst_ref=target.at[step],
            send_sem=give_sem.at[part, step],
            recv_sem=take_sem.at[part, step],
            device_id={"sec": sec, "img": peer},
            device_id_type=MESH,
        )

    pieces = range(len(spans))

    def send(turn, which, part):
        @pl.when(not_bottom)
        def _():
            hop(turn, which, part).start()

    def chain_five(turn):
        for part in pieces:
            arrive(turn, 1, part)
            through_five(turn, outbox.at[turn, 0], spans[part])
            send(turn, 0, part)

    def chain_three(turn):
        for part in pieces:
            through_three(turn, outbox.at[turn, 1], spans[part])
            send(turn, 1, part)

    def add_points(turn):
        held = lax.rem(turn, 2)
        add_point(turn, mixed_three.at[held], total_three)
        add_point(turn, mixed_five.at[held], total_five)

    def finish_points():
        for part in pieces:
            arrive(end, 0, part)
        for part, mixed, total, give in (
            (0, mixed_three, total_three, give_three),
            (1, mixed_five, total_five, give_five),
        ):
            add_point(end, mixed.at[end % 2], total)
            for peer in range(group):
                give[peer] = (total[peer * rows : (peer + 1) * rows] * factor).astype(BF16)
            start_share(part)

    side = img // 2
    mate = img + 1 - 2 * (img % 2)
    far_inner, far_outer = 2 - side, 3 - 3 * side
    inner = (img + 1) // 2 % 2 == 1
    outer = (img + 1) // 2 % 2 == 0

    def pass_on(part, source, slot, sender, peer):
        target = (take_three, take_five)[part]
        return pltpu.make_async_remote_copy(
            src_ref=source,
            dst_ref=target.at[slot],
            send_sem=give_sem.at[part, sender],
            recv_sem=take_sem.at[part, slot],
            device_id={"sec": sec, "img": peer},
            device_id_type=MESH,
        )

    def start_share(part):
        give = (give_three, give_five)[part]
        if not folded:
            for step in range(1, group):
                share(part, step).start()
            return

        @pl.when(outer)
        def _():
            pass_on(part, give.at[far_outer], 0, 0, mate).start()
            pass_on(part, give.at[far_inner], 1, 1, mate).start()

        pass_on(part, give.at[mate], 2, 2, mate).start()

    def relay(part):
        if not folded:
            return
        give, take = ((give_three, take_three), (give_five, take_five))[part]
        held = (relay_three, relay_five)[part]

        @pl.when(inner)
        def _():
            for slot, peer in ((0, far_outer), (1, far_inner)):
                pass_on(part, give.at[peer], slot, slot, mate).wait_recv()
                held[slot] = (give[peer].astype(F32) + take[slot].astype(F32)).astype(BF16)
                pass_on(part, held.at[slot], 3, slot, peer).start()

    prepare(0)
    point_both[0:channels] = point_five[...]
    point_both[channels:] = point_three[...]
    for ref in (
        parts_five,
        parts_three,
        folds_five,
        folds_three,
        sums_five,
        sums_three,
        total_five,
        total_three,
        sums_all,
    ):
        ref[...] = jnp.zeros(ref.shape, ref.dtype)
    callers = group + 1 - bottom.astype(jnp.int32) - top.astype(jnp.int32)
    pl.semaphore_wait(barrier, callers)
    first_copy(0).wait()
    first_copy(1).wait()

    def turn_work(turn, carry):
        for part in pieces:
            arrive(turn, 0, part)
        pull(turn)
        chain_five(turn)
        chain_three(turn)
        prepare(turn + 1)

        def ahead(later, carry):
            forward(later, (0, pairs))
            return carry

        lax.fori_loop(turn + lax.min(turn, 1), turn + 2, ahead, 0)
        add_points(turn)
        return carry

    lax.fori_loop(0, end, turn_work, 0)
    finish_points()
    pull(end)

    def all_taps(turn, carry):
        @pl.when(turn == turns // 2)
        def _():
            relay(0)

        add_taps(turn)
        return carry

    lax.fori_loop(0, turns, all_taps, 0)
    relay(1)
    count_five, count_three = five * five, three * three
    for sums, start, count in ((sums_five, 0, count_five), (sums_three, count_five, count_three)):
        sums_all[start : start + count] = sums[0:count, 0:channels] + sums[0:count, channels:]
    flipped = sums_all[...].T * factor
    for peer in range(group):
        own = flipped[peer * rows : (peer + 1) * rows].T
        give_taps[peer] = own[0 : give_taps.shape[1]].astype(BF16)
    for step in range(1, group):
        share(2, step).start()
    for part in range(len(spans)):
        arrive(end, 1, part)
    compact_five(end, final.at[0], (0, pairs))
    compact_three(end, final.at[1], (0, pairs))
    finals = [
        pltpu.make_async_copy(
            final.at[which, pl.ds(0, height)], outgoing.at[which], final_sem.at[which]
        )
        for which in range(2)
    ]
    for copy in finals:
        copy.start()

    def gathered(part, give, take):
        value = give[img].astype(F32)
        if folded and part < 2:
            for slot in (2, 3):
                pass_on(part, give.at[mate], slot, 2, mate).wait_recv()
                value = value + take[slot].astype(F32)
            return value
        for step in range(1, group):
            share(part, step).wait_recv()
            value = value + take[step].astype(F32)
        return value

    out_three[...] = gathered(0, give_three, take_three)
    out_five[...] = gathered(1, give_five, take_five)
    by_tap = gathered(2, give_taps, take_taps)
    for tap in range(count_five):
        out_taps_five[tap] = by_tap[tap : tap + 1]
    for tap in range(count_three):
        out_taps_three[tap] = by_tap[count_five + tap : count_five + tap + 1]
    for part in range(3):
        for step in range(1, group):
            if folded and part < 2:
                source = (give_three, give_five)[part].at[mate]
                pass_on(part, source, 2, step - 1, mate).wait_send()
            else:
                share(part, step).wait_send()
    for copy in finals:
        copy.wait()

    @pl.when(not_bottom)
    def _():
        for turn in range(end):
            for which in range(2):
                for part in range(len(spans)):
                    hop(turn, which, part).wait_send()


def local(
    sections,
    group,
    saved_last,
    saved_older,
    arriving,
    head_adjoint,
    plan,
    depth_five,
    depth_three,
    point_five,
    point_three,
):
    turns, _, height, width, channels = saved_last.shape[1:]
    count_five, count_three = depth_five.shape[1], depth_three.shape[1]
    five, three = round(count_five**0.5), round(count_three**0.5)
    breadth = up(width + five // 2, 8)
    pairs = up(height, 2) // 2
    even = pltpu.VMEM((turns, pairs + 2, breadth, 2 * channels), BF16)
    odd = pltpu.VMEM((turns, pairs + 1, breadth, 2 * channels), BF16)
    rows = channels // group
    chunk = -(-pairs // CHUNKS)
    spans = tuple((at, min(at + chunk, pairs)) for at in range(0, pairs, chunk))
    vmem = pl.BlockSpec(memory_space=pltpu.VMEM)
    smem = pl.BlockSpec(memory_space=pltpu.SMEM)
    outside = pl.BlockSpec(memory_space=pl.ANY)
    body = functools.partial(kernel_body, sections, group, (five, three), spans)
    grow = (0, breadth - width)
    outgoing, grad_five, grad_three, taps_five, taps_three = pl.pallas_call(
        body,
        out_shape=(
            jax.ShapeDtypeStruct((2, height, width, channels), BF16),
            jax.ShapeDtypeStruct((rows, channels), F32),
            jax.ShapeDtypeStruct((rows, channels), F32),
            jax.ShapeDtypeStruct((count_five, 1, rows), F32),
            jax.ShapeDtypeStruct((count_three, 1, rows), F32),
        ),
        in_specs=[smem, vmem, vmem, *[outside] * 2, *[vmem] * 10],
        out_specs=(outside, *[vmem] * 4),
        scratch_shapes=[
            pltpu.VMEM((turns, 2, 2 * pairs, breadth, channels), BF16),
            pltpu.VMEM((turns - 1, 2, 2 * pairs, breadth, channels), BF16),
            pltpu.VMEM((2, 2 * pairs, width, channels), BF16),
            *([even, odd] * 4),
            pltpu.VMEM((2, 2 * pairs, breadth, channels), BF16),
            pltpu.VMEM((2, 2 * pairs, breadth, channels), BF16),
            pltpu.VMEM((2, TWO * LANES, 2 * channels), BF16),
            pltpu.VMEM((2, TWO * LANES, 2 * channels), BF16),
            pltpu.VMEM((2 * channels, channels), BF16),
            pltpu.VMEM((2, up(count_five * 8, LANES), 2 * channels), BF16),
            pltpu.VMEM((2, up(count_three * 8, LANES), 2 * channels), BF16),
            pltpu.VMEM((count_five, 8, 2 * channels), BF16),
            pltpu.VMEM((count_three, 8, 2 * channels), BF16),
            pltpu.VMEM((channels, channels), F32),
            pltpu.VMEM((channels, channels), F32),
            pltpu.VMEM((up(count_five, 8), 2 * channels), F32),
            pltpu.VMEM((up(count_three, 8), 2 * channels), F32),
            pltpu.VMEM((LANES, channels), F32),
            pltpu.VMEM((group, rows, channels), BF16),
            pltpu.VMEM((group, rows, channels), BF16),
            pltpu.VMEM((group, up(count_five + count_three, 16), rows), BF16),
            pltpu.VMEM((group, rows, channels), BF16),
            pltpu.VMEM((group, rows, channels), BF16),
            pltpu.VMEM((group, up(count_five + count_three, 16), rows), BF16),
            pltpu.VMEM((2, rows, channels), BF16),
            pltpu.VMEM((2, rows, channels), BF16),
            pltpu.SemaphoreType.DMA((turns, 2)),
            pltpu.SemaphoreType.DMA((turns - 1, 2, len(spans))),
            pltpu.SemaphoreType.DMA((turns - 1, 2, len(spans))),
            pltpu.SemaphoreType.DMA((3, group)),
            pltpu.SemaphoreType.DMA((3, group)),
            pltpu.SemaphoreType.DMA((2,)),
        ],
        compiler_params=pltpu.CompilerParams(
            collective_id=0, has_side_effects=True, vmem_limit_bytes=GRANT
        ),
    )(
        plan,
        saved_last.reshape(turns, height, width, channels),
        saved_older.reshape(turns, height, width, channels),
        jnp.pad(arriving[0, :, 0], ((0, 0), (0, 0), grow, (0, 0))),
        jnp.pad(head_adjoint[:, :, 0], ((0, 0), (0, 0), (0, 0), grow, (0, 0))),
        depth_five[0],
        depth_three[0],
        point_five[0],
        point_three[0],
        *(
            selection(breadth, width, kernel, back)
            for back in (False, True)
            for kernel in (five, three)
        ),
        *(gathering(count) for count in (count_five, count_three)),
    )
    return (
        outgoing.reshape(1, 2, 1, height, width, channels),
        grad_five[None],
        taps_five.transpose(1, 2, 0),
        grad_three[None],
        taps_three.transpose(1, 2, 0),
    )


def solution(mesh):
    placed = (
        P("sec", None, "img", None, None, None),
        P("sec", None, "img", None, None, None),
        P("sec", None, "img", None, None, None),
        P(None, None, "img", None, None, None),
        P("sec", None),
        P("sec", None, None),
        P("sec", None, None),
        P("sec", None, None),
        P("sec", None, None),
    )
    return jax.shard_map(
        functools.partial(local, mesh.shape["sec"], mesh.shape["img"]),
        mesh=mesh,
        in_specs=placed,
        out_specs=(
            P("sec", None, "img", None, None, None),
            P("sec", "img", None),
            P("sec", "img", None),
            P("sec", "img", None),
            P("sec", "img", None),
        ),
        check_vma=False,
    )
```

```python
import functools

import jax
import jax.numpy as jnp
import numpy as np
from jax import lax
from jax.experimental import pallas as pl
from jax.experimental.pallas import tpu as pltpu
from jax.sharding import PartitionSpec as P

F32 = jnp.float32
BF16 = jnp.bfloat16
LANES = 128
WIDE = 256
MESH = pl.DeviceIdType.MESH
TWO = 2
CHUNKS = 3
GRANT = 36 * 2**20


def up(value, unit):
    return -(-value // unit) * unit


def turned(block, shift):
    shift = shift % block.shape[0]
    return block if shift == 0 else pltpu.roll(block, shift, 0)


def rows_at(even, odd, pair, offset, lanes):
    if offset % 2 == 0:
        block = even[pair + offset // 2 + 1, :, lanes]
    else:
        block = odd[pair + (offset + 1) // 2, :, lanes]
    return block.reshape(-1, 8, WIDE)


def rolled(even, odd, taps, kernel, pair, lanes, back):
    radius = kernel // 2
    held = [rows_at(even, odd, pair, k - radius, lanes) for k in range(kernel)]
    total = None
    for col_tap in range(kernel):
        part = None
        for row_tap in range(kernel):
            at = kernel - 1 - row_tap if back else row_tap
            term = taps[row_tap * kernel + col_tap, :, lanes][None] * held[at]
            part = term if part is None else part + term
        wide = part.astype(F32).reshape(-1, WIDE)
        moved = turned(wide, col_tap - radius if back else radius - col_tap)
        total = moved if total is None else total + moved
    return total


def filtered(even, odd, taps, kernel, group, select, parts, back):
    radius = kernel // 2
    breadth, wides = even.shape[1:]
    for slot, pair in enumerate(group):
        for first in range(0, wides, WIDE):
            lanes = slice(first, first + WIDE)
            held = [rows_at(even, odd, pair, k - radius, lanes) for k in range(kernel)]
            for col_tap in range(kernel):
                part = None
                for row_tap in range(kernel):
                    at = kernel - 1 - row_tap if back else row_tap
                    term = taps[row_tap * kernel + col_tap, :, lanes][None] * held[at]
                    part = term if part is None else part + term
                at = slot * LANES + col_tap * breadth
                parts[at : at + breadth, lanes] = part.reshape(breadth, WIDE)
    return lax.dot_general(
        select[...], parts[...], (((1,), (0,)), ((), ())), preferred_element_type=F32
    )


def selection(breadth, width, kernel, back):
    table = np.zeros((TWO * breadth, TWO * LANES), np.float32)
    for slot in range(TWO):
        for col_tap in range(kernel):
            shift = kernel // 2 - col_tap if back else col_tap - kernel // 2
            for col in range(width):
                if 0 <= col + shift < width:
                    at = slot * LANES + col_tap * breadth + col + shift
                    table[slot * breadth + col, at] = 1.0
    return jnp.asarray(table, BF16)


def tap_folds(even, odd, back, folds, kernel, pair):
    radius = kernel // 2
    breadth, wides = even.shape[1:]
    for first in range(0, wides, WIDE):
        lanes = slice(first, first + WIDE)
        held = [rows_at(even, odd, pair, k - radius, lanes) for k in range(kernel)]
        wide = back[pair + 1, :, lanes].astype(F32)
        for col_tap in range(kernel):
            other = turned(wide, col_tap - radius).astype(BF16).reshape(-1, 8, WIDE)
            for row_tap in range(kernel):
                term = held[row_tap] * other
                folded = term[0]
                for part in range(1, term.shape[0]):
                    folded = folded + term[part]
                tap = row_tap * kernel + col_tap
                folds[tap * 8 : tap * 8 + 8, lanes] = folded


def gathering(count):
    table = np.zeros((up(count, 8), up(count * 8, LANES)), np.float32)
    for tap in range(count):
        table[tap, tap * 8 : tap * 8 + 8] = 1.0
    return jnp.asarray(table, BF16)


def selection(breadth, width, kernel, back):
    table = np.zeros((TWO * breadth, TWO * LANES), np.float32)
    for slot in range(TWO):
        for col_tap in range(kernel):
            shift = kernel // 2 - col_tap if back else col_tap - kernel // 2
            for col in range(width):
                if 0 <= col + shift < width:
                    at = slot * LANES + col_tap * breadth + col + shift
                    table[slot * breadth + col, at] = 1.0
    return jnp.asarray(table, BF16)


def tap_sums(even, odd, back, sums, kernel, pair, lanes):
    radius = kernel // 2
    held = [rows_at(even, odd, pair, k - radius, lanes) for k in range(kernel)]
    wide = back[pair + 1, :, lanes].astype(F32)
    for col_tap in range(kernel):
        moved = turned(wide, col_tap - radius).astype(BF16).reshape(-1, 8, WIDE)
        for row_tap in range(kernel):
            term = held[row_tap] * moved
            folded = term[0]
            for part in range(1, term.shape[0]):
                folded = folded + term[part]
            tap = row_tap * kernel + col_tap
            sums[tap, :, lanes] = sums[tap, :, lanes] + folded.astype(F32)


def kernel_body(
    sections,
    group,
    kernels,
    spans,
    plan,
    last,
    older,
    arriving,
    head,
    depth_five,
    depth_three,
    point_five,
    point_three,
    select_five,
    select_three,
    select_five_back,
    select_three_back,
    gather_five,
    gather_three,
    outgoing,
    out_points,
    out_taps,
    inbox,
    outbox,
    final,
    even_last,
    odd_last,
    even_older,
    odd_older,
    even_five,
    odd_five,
    even_three,
    odd_three,
    mixed_five,
    mixed_three,
    parts_five,
    parts_three,
    point_both,
    folds_five,
    folds_three,
    taps_five,
    taps_three,
    total_five,
    total_three,
    sums_five,
    sums_three,
    sums_all,
    give_five,
    give_three,
    give_taps,
    take_five,
    take_three,
    take_taps,
    relay_three,
    relay_five,
    local_sem,
    send_sem,
    recv_sem,
    give_sem,
    take_sem,
    final_sem,
    weight_sem,
):
    five, three = kernels
    turns, height, width, channels = last.shape
    breadth = inbox.shape[3]
    rows = channels // group
    pairs = spans[-1][1]
    blocks = 2 * channels // WIDE
    columns = channels // LANES
    end = turns - 1
    folded = group == 4
    sec = lax.axis_index("sec")
    img = lax.axis_index("img")
    top = sec == sections - 1
    bottom = sec == 0
    not_top = sec < sections - 1
    not_bottom = sec > 0

    def lines(span):
        return 2 * span[0], min(2 * span[1], height)

    def first_copy(which):
        target = inbox.at[0, which, pl.ds(0, height)]
        return pltpu.make_async_copy(arriving.at[which], target, local_sem.at[which])

    def take_head(turn):
        edge = jnp.zeros((breadth - width, channels), F32)

        def one(row, carry):
            both = head[turn - 1, row].astype(F32)
            for which in range(2):
                own = both[:, which]
                inbox[turn, which, row] = jnp.concatenate([own, edge], 0).astype(BF16)
            return carry

        lax.fori_loop(0, height, one, 0, unroll=3)

    weights = [
        pltpu.make_async_copy(
            source, point_both.at[pl.ds(at * channels, channels)], weight_sem.at[at]
        )
        for at, source in enumerate((point_five, point_three))
    ]
    for which in range(2):
        first_copy(which).start()
        weights[which].start()

    barrier = pltpu.get_barrier_semaphore()
    for step in range(1, group):
        pl.semaphore_signal(
            barrier,
            inc=1,
            device_id={"sec": sec, "img": lax.rem(img + step, group)},
            device_id_type=MESH,
        )

    @pl.when(not_bottom)
    def _():
        pl.semaphore_signal(
            barrier, inc=1, device_id={"sec": sec - 1, "img": img}, device_id_type=MESH
        )

    @pl.when(not_top)
    def _():
        pl.semaphore_signal(
            barrier, inc=1, device_id={"sec": sec + 1, "img": img}, device_id_type=MESH
        )

    edge_even = jnp.zeros(even_five.shape[2:], BF16)

    def clear(turn, carry):
        for ref in (even_last, even_older, even_five, even_three):
            ref[turn, 0] = edge_even
            ref[turn, pairs + 1] = edge_even
        for ref in (odd_last, odd_older, odd_five, odd_three):
            ref[turn, pairs] = edge_even
        return carry

    lax.fori_loop(0, turns, clear, 0)
    for wide, packed in ((depth_five, taps_five), (depth_three, taps_three)):
        for tap in range(packed.shape[0]):
            value = jnp.broadcast_to(wide[tap : tap + 1].astype(F32), (8, channels))
            packed[tap] = jnp.concatenate([value, value], 1).astype(BF16)

    def prepare(turn):
        slot = plan[0, turn]
        zeros = jnp.zeros((breadth, channels), BF16)
        edge = jnp.zeros((breadth - width, channels), F32)
        for saved, even, odd in ((last, even_last, odd_last), (older, even_older, odd_older)):
            for row in range(-1, 2 * pairs):
                inside = 0 <= row < height
                active = zeros
                if inside:
                    raised = jnp.maximum(saved[slot, row], 0).astype(F32)
                    active = jnp.concatenate([raised, edge], 0).astype(BF16)
                lanes = slice((row % 2) * channels, (row % 2 + 1) * channels)
                if row >= 0:
                    even[turn, row // 2 + 1, :, lanes] = active
                if row < 2 * pairs - 1:
                    lanes = slice((1 - row % 2) * channels, (2 - row % 2) * channels)
                    odd[turn, (row + 1) // 2, :, lanes] = active

    def hop(turn, which, part):
        start, stop = lines(spans[part])
        return pltpu.make_async_remote_copy(
            src_ref=outbox.at[turn, which, pl.ds(start, stop - start)],
            dst_ref=inbox.at[turn + 1, which, pl.ds(start, stop - start)],
            send_sem=send_sem.at[turn, which, part],
            recv_sem=recv_sem.at[turn, which, part],
            device_id={"sec": lax.max(sec - 1, 0), "img": img},
            device_id_type=MESH,
        )

    def arrive(turn, which, part):
        if which == 0 and part == 0:

            @pl.when(jnp.logical_and(turn > 0, top))
            def _():
                take_head(turn)

        @pl.when(jnp.logical_and(turn > 0, not_top))
        def _():
            hop(turn - 1, which, part).wait_recv()

    def pull(turn):
        grad = inbox[turn, 0, 0:height].reshape(-1, channels)
        product = lax.dot_general(
            grad, point_both[...], (((1,), (1,)), ((), ())), preferred_element_type=F32
        )
        for even, odd, first in (
            (even_five, odd_five, 0),
            (even_three, odd_three, channels),
        ):

            def line(row):
                if 0 <= row < height:
                    at = row * breadth
                    return product[at : at + breadth, first : first + channels].astype(BF16)
                return jnp.zeros((breadth, channels), BF16)

            for pair in range(pairs):
                for side in range(2):
                    lanes = slice(side * channels, (side + 1) * channels)
                    even[turn, pair + 1, :, lanes] = line(2 * pair + side)
                    odd[turn, pair, :, lanes] = line(2 * pair - 1 + side)

    def parts(pair, block):
        for part in range(WIDE // LANES):
            at = block * (WIDE // LANES) + part
            lanes = slice((at % columns) * LANES, (at % columns + 1) * LANES)
            yield 2 * pair + at // columns, lanes, slice(part * LANES, (part + 1) * LANES)

    def each_block(work, span):
        def one(pair, carry):
            for block in range(blocks):
                work(pair, block, slice(block * WIDE, (block + 1) * WIDE))
            return carry

        lax.fori_loop(span[0], span[1], one, 0)

    def compact_five(turn, target, span):
        wide_to = target.shape[1]

        def work(pair, block, wide):
            out = rolled(
                even_five.at[turn], odd_five.at[turn], taps_five, five, pair, wide, True
            )
            kept = jnp.where(even_last[turn, pair + 1, :, wide].astype(F32) > 0, out, 0.0)
            for at, lanes, cut in parts(pair, block):
                own = inbox[turn, 0, at, :, lanes].astype(F32)
                extra = inbox[turn, 1, at, :, lanes].astype(F32)
                done = kept[:, cut] + own + extra
                target[at, :, lanes] = done[0:wide_to].astype(BF16)

        each_block(work, span)

    def compact_three(turn, target, span):
        wide_to = target.shape[1]

        def work(pair, block, wide):
            out = rolled(
                even_three.at[turn], odd_three.at[turn], taps_three, three, pair, wide, True
            )
            kept = jnp.where(even_older[turn, pair + 1, :, wide].astype(F32) > 0, out, 0.0)
            for at, lanes, cut in parts(pair, block):
                target[at, :, lanes] = kept[0:wide_to, cut].astype(BF16)

        each_block(work, span)

    def groups(span):
        for count, first in enumerate(range(span[0], span[1], TWO)):
            yield count % 2, range(first, min(first + TWO, span[1]))

    def sides(group, out):
        for slot, pair in enumerate(group):
            for side in range(2):
                lanes = slice(side * channels, (side + 1) * channels)
                at = slot * breadth
                yield pair, 2 * pair + side, lanes, out[at : at + breadth, lanes]

    def through_five(turn, target, span):
        wide_to = target.shape[1]
        for odds, group in groups(span):
            out = filtered(
                even_five.at[turn],
                odd_five.at[turn],
                taps_five,
                five,
                group,
                select_five_back,
                parts_five.at[odds],
                True,
            )
            for pair, row, lanes, value in sides(group, out):
                kept = jnp.where(even_last[turn, pair + 1, :, lanes].astype(F32) > 0, value, 0.0)
                own = inbox[turn, 0, row].astype(F32)
                extra = inbox[turn, 1, row].astype(F32)
                target[row] = (kept + own + extra)[0:wide_to].astype(BF16)

    def through_three(turn, target, span):
        wide_to = target.shape[1]
        for odds, group in groups(span):
            out = filtered(
                even_three.at[turn],
                odd_three.at[turn],
                taps_three,
                three,
                group,
                select_three_back,
                parts_three.at[odds],
                True,
            )
            for pair, row, lanes, value in sides(group, out):
                kept = jnp.where(even_older[turn, pair + 1, :, lanes].astype(F32) > 0, value, 0.0)
                target[row] = kept[0:wide_to].astype(BF16)

    def forward(turn, span):
        for odds, group in groups(span):
            for even, odd, taps, mixed, kernel, select, held in (
                (even_last, odd_last, taps_five, mixed_five, five, select_five, parts_five),
                (even_older, odd_older, taps_three, mixed_three, three, select_three, parts_three),
            ):
                out = filtered(
                    even.at[turn], odd.at[turn], taps, kernel, group, select, held.at[odds], False
                )
                for pair, row, lanes, value in sides(group, out):
                    mixed[lax.rem(turn, 2), row] = value.astype(BF16)

    def add_taps(turn):
        for pair in range(pairs):
            for even, odd, back, folds, gathers, sums, kernel in (
                (even_last, odd_last, even_five, folds_five, gather_five, sums_five, five),
                (even_older, odd_older, even_three, folds_three, gather_three, sums_three, three),
            ):
                held = folds.at[pair % 2]
                tap_folds(even.at[turn], odd.at[turn], back.at[turn], held, kernel, pair)
                sums[...] += jnp.dot(gathers[...], held[...], preferred_element_type=F32)

    def add_point(turn, mixed, total):
        flat = mixed[0:height].reshape(-1, channels)
        grad = inbox[turn, 0, 0:height].reshape(-1, channels)
        total[...] += lax.dot_general(
            flat, grad, (((0,), (0,)), ((), ())), preferred_element_type=F32
        )

    def share(part, step):
        source = (give_three, give_five, give_taps)[part]
        target = (take_three, take_five, take_taps)[part]
        peer = lax.rem(img + step, group)
        return pltpu.make_async_remote_copy(
            src_ref=source.at[peer],
            dst_ref=target.at[step],
            send_sem=give_sem.at[part, step],
            recv_sem=take_sem.at[part, step],
            device_id={"sec": sec, "img": peer},
            device_id_type=MESH,
        )

    pieces = range(len(spans))

    def send(turn, which, part):
        @pl.when(not_bottom)
        def _():
            hop(turn, which, part).start()

    def chain_five(turn):
        for part in pieces:
            arrive(turn, 1, part)
            through_five(turn, outbox.at[turn, 0], spans[part])
            send(turn, 0, part)

    def chain_three(turn):
        for part in pieces:
            through_three(turn, outbox.at[turn, 1], spans[part])
            send(turn, 1, part)

    def add_points(turn):
        held = lax.rem(turn, 2)
        add_point(turn, mixed_three.at[held], total_three)
        add_point(turn, mixed_five.at[held], total_five)

    def finish_points():
        for part in pieces:
            arrive(end, 0, part)
        for part, mixed, total, give in (
            (0, mixed_three, total_three, give_three),
            (1, mixed_five, total_five, give_five),
        ):
            add_point(end, mixed.at[end % 2], total)
            for peer in range(group):
                give[peer] = total[peer * rows : (peer + 1) * rows].astype(BF16)
            start_share(part)

        if folded:

            @pl.when(outer)
            def _():
                pass_on(0, give_three.at[mate], 2, 2, mate).start()
                pass_on(1, give_five.at[mate], 2, 2, mate).start()

    side = img // 2
    mate = img + 1 - 2 * (img % 2)
    far_inner, far_outer = 2 - side, 3 - 3 * side
    inner = (img + 1) // 2 % 2 == 1
    outer = (img + 1) // 2 % 2 == 0

    def pass_on(part, source, slot, sender, peer):
        target = (take_three, take_five)[part]
        return pltpu.make_async_remote_copy(
            src_ref=source,
            dst_ref=target.at[slot],
            send_sem=give_sem.at[part, sender],
            recv_sem=take_sem.at[part, slot],
            device_id={"sec": sec, "img": peer},
            device_id_type=MESH,
        )

    def start_share(part):
        give = (give_three, give_five)[part]
        if not folded:
            for step in range(1, group):
                share(part, step).start()
            return

        @pl.when(outer)
        def _():
            pass_on(part, give.at[far_outer], 0, 0, mate).start()
            pass_on(part, give.at[far_inner], 1, 1, mate).start()

        @pl.when(inner)
        def _():
            pass_on(part, give.at[mate], 2, 2, mate).start()

    def relay(part):
        if not folded:
            return
        give, take = ((give_three, take_three), (give_five, take_five))[part]
        held = (relay_three, relay_five)[part]

        @pl.when(inner)
        def _():
            for slot, peer in ((0, far_outer), (1, far_inner)):
                pass_on(part, give.at[peer], slot, slot, mate).wait_recv()
                held[slot] = (give[peer].astype(F32) + take[slot].astype(F32)).astype(BF16)
                pass_on(part, held.at[slot], 3, slot, peer).start()

    prepare(0)
    for ref in (parts_five, parts_three):
        ref[...] = jnp.zeros(ref.shape, ref.dtype)
    callers = group + 1 - bottom.astype(jnp.int32) - top.astype(jnp.int32)
    pl.semaphore_wait(barrier, callers)
    for which in range(2):
        first_copy(which).wait()
        weights[which].wait()

    def turn_work(turn, carry):
        for part in pieces:
            arrive(turn, 0, part)
        pull(turn)
        chain_five(turn)
        chain_three(turn)

        @pl.when(turn == 0)
        def _():
            for ref in (
                folds_five,
                folds_three,
                sums_five,
                sums_three,
                total_five,
                total_three,
                sums_all,
            ):
                ref[...] = jnp.zeros(ref.shape, ref.dtype)

        prepare(turn + 1)

        def ahead(later, carry):
            forward(later, (0, pairs))
            return carry

        lax.fori_loop(turn + lax.min(turn, 1), turn + 2, ahead, 0)
        add_points(turn)
        return carry

    lax.fori_loop(0, end, turn_work, 0)
    finish_points()
    pull(end)

    def all_taps(turn, carry):
        @pl.when(turn == turns // 2)
        def _():
            relay(0)

        add_taps(turn)
        return carry

    lax.fori_loop(0, turns, all_taps, 0)
    relay(1)
    count_five, count_three = five * five, three * three
    for sums, start, count in ((sums_five, 0, count_five), (sums_three, count_five, count_three)):
        sums_all[start : start + count] = sums[0:count, 0:channels] + sums[0:count, channels:]
    flipped = sums_all[...].T
    for peer in range(group):
        own = flipped[peer * rows : (peer + 1) * rows].T
        give_taps[peer] = own[0 : give_taps.shape[1]].astype(BF16)
    for step in range(1, group):
        share(2, step).start()
    for part in range(len(spans)):
        arrive(end, 1, part)
    compact_five(end, final.at[0], (0, pairs))
    compact_three(end, final.at[1], (0, pairs))
    finals = [
        pltpu.make_async_copy(
            final.at[which, pl.ds(0, height)], outgoing.at[which], final_sem.at[which]
        )
        for which in range(2)
    ]
    for copy in finals:
        copy.start()

    def gathered(part, give, take):
        value = give[img].astype(F32)
        if folded and part < 2:
            for slot in (2, 3):
                pass_on(part, give.at[mate], slot, 2, mate).wait_recv()
                value = value + take[slot].astype(F32)
            return value
        for step in range(1, group):
            share(part, step).wait_recv()
            value = value + take[step].astype(F32)
        return value

    out_points[1] = gathered(0, give_three, take_three)
    out_points[0] = gathered(1, give_five, take_five)
    by_tap = gathered(2, give_taps, take_taps)
    for tap in range(count_five + count_three):
        out_taps[tap] = by_tap[tap : tap + 1]
    for part in range(3):
        for step in range(1, group):
            if folded and part < 2:
                source = (give_three, give_five)[part].at[mate]
                pass_on(part, source, 2, step - 1, mate).wait_send()
            else:
                share(part, step).wait_send()
    for copy in finals:
        copy.wait()

    @pl.when(not_bottom)
    def _():
        for turn in range(end):
            for which in range(2):
                for part in range(len(spans)):
                    hop(turn, which, part).wait_send()


def scale_body(factor, points, taps, five, three, taps_five, taps_three):
    count = taps_five.shape[0]
    five[...] = points[0] * factor
    three[...] = points[1] * factor
    taps_five[...] = taps[0:count] * factor
    taps_three[...] = taps[count:] * factor


def local(
    sections,
    group,
    saved_last,
    saved_older,
    arriving,
    head_adjoint,
    plan,
    depth_five,
    depth_three,
    point_five,
    point_three,
):
    turns, _, height, width, channels = saved_last.shape[1:]
    count_five, count_three = depth_five.shape[1], depth_three.shape[1]
    five, three = round(count_five**0.5), round(count_three**0.5)
    breadth = up(width + five // 2, 8)
    pairs = up(height, 2) // 2
    even = pltpu.VMEM((turns, pairs + 2, breadth, 2 * channels), BF16)
    odd = pltpu.VMEM((turns, pairs + 1, breadth, 2 * channels), BF16)
    rows = channels // group
    factor = 1.0 / (height * width)
    chunk = -(-pairs // CHUNKS)
    spans = tuple((at, min(at + chunk, pairs)) for at in range(0, pairs, chunk))
    vmem = pl.BlockSpec(memory_space=pltpu.VMEM)
    smem = pl.BlockSpec(memory_space=pltpu.SMEM)
    outside = pl.BlockSpec(memory_space=pl.ANY)
    fixed = pl.BlockSpec(memory_space=pltpu.HBM)
    body = functools.partial(kernel_body, sections, group, (five, three), spans)
    grow = (0, breadth - width)
    outgoing, points, taps = pl.pallas_call(
        body,
        out_shape=(
            jax.ShapeDtypeStruct((2, height, width, channels), BF16),
            jax.ShapeDtypeStruct((2, rows, channels), F32),
            jax.ShapeDtypeStruct((count_five + count_three, 1, rows), F32),
        ),
        in_specs=[smem, vmem, vmem, outside, vmem, *[vmem] * 2, *[fixed] * 2, *[vmem] * 6],
        out_specs=(outside, *[vmem] * 2),
        scratch_shapes=[
            pltpu.VMEM((turns, 2, 2 * pairs, breadth, channels), BF16),
            pltpu.VMEM((turns - 1, 2, 2 * pairs, breadth, channels), BF16),
            pltpu.VMEM((2, 2 * pairs, width, channels), BF16),
            *([even, odd] * 4),
            pltpu.VMEM((2, 2 * pairs, breadth, channels), BF16),
            pltpu.VMEM((2, 2 * pairs, breadth, channels), BF16),
            pltpu.VMEM((2, TWO * LANES, 2 * channels), BF16),
            pltpu.VMEM((2, TWO * LANES, 2 * channels), BF16),
            pltpu.VMEM((2 * channels, channels), BF16),
            pltpu.VMEM((2, up(count_five * 8, LANES), 2 * channels), BF16),
            pltpu.VMEM((2, up(count_three * 8, LANES), 2 * channels), BF16),
            pltpu.VMEM((count_five, 8, 2 * channels), BF16),
            pltpu.VMEM((count_three, 8, 2 * channels), BF16),
            pltpu.VMEM((channels, channels), F32),
            pltpu.VMEM((channels, channels), F32),
            pltpu.VMEM((up(count_five, 8), 2 * channels), F32),
            pltpu.VMEM((up(count_three, 8), 2 * channels), F32),
            pltpu.VMEM((LANES, channels), F32),
            pltpu.VMEM((group, rows, channels), BF16),
            pltpu.VMEM((group, rows, channels), BF16),
            pltpu.VMEM((group, up(count_five + count_three, 16), rows), BF16),
            pltpu.VMEM((group, rows, channels), BF16),
            pltpu.VMEM((group, rows, channels), BF16),
            pltpu.VMEM((group, up(count_five + count_three, 16), rows), BF16),
            pltpu.VMEM((2, rows, channels), BF16),
            pltpu.VMEM((2, rows, channels), BF16),
            pltpu.SemaphoreType.DMA((2,)),
            pltpu.SemaphoreType.DMA((turns - 1, 2, len(spans))),
            pltpu.SemaphoreType.DMA((turns - 1, 2, len(spans))),
            pltpu.SemaphoreType.DMA((3, group)),
            pltpu.SemaphoreType.DMA((3, group)),
            pltpu.SemaphoreType.DMA((2,)),
            pltpu.SemaphoreType.DMA((2,)),
        ],
        compiler_params=pltpu.CompilerParams(
            collective_id=0, has_side_effects=True, vmem_limit_bytes=GRANT
        ),
    )(
        plan,
        saved_last.reshape(turns, height, width, channels),
        saved_older.reshape(turns, height, width, channels),
        jnp.pad(arriving[0, :, 0], ((0, 0), (0, 0), grow, (0, 0))),
        head_adjoint[:, :, 0].transpose(0, 2, 3, 1, 4),
        depth_five[0],
        depth_three[0],
        point_five[0],
        point_three[0],
        *(
            selection(breadth, width, kernel, back)
            for back in (False, True)
            for kernel in (five, three)
        ),
        *(gathering(count) for count in (count_five, count_three)),
    )
    grad_five, grad_three, taps_five, taps_three = pl.pallas_call(
        functools.partial(scale_body, factor),
        out_shape=(
            jax.ShapeDtypeStruct((rows, channels), F32),
            jax.ShapeDtypeStruct((rows, channels), F32),
            jax.ShapeDtypeStruct((count_five, 1, rows), F32),
            jax.ShapeDtypeStruct((count_three, 1, rows), F32),
        ),
        in_specs=[vmem, vmem],
        out_specs=(vmem,) * 4,
        compiler_params=pltpu.CompilerParams(vmem_limit_bytes=GRANT),
    )(points, taps)
    return (
        outgoing.reshape(1, 2, 1, height, width, channels),
        grad_five[None],
        taps_five.transpose(1, 2, 0),
        grad_three[None],
        taps_three.transpose(1, 2, 0),
    )


def solution(mesh):
    placed = (
        P("sec", None, "img", None, None, None),
        P("sec", None, "img", None, None, None),
        P("sec", None, "img", None, None, None),
        P(None, None, "img", None, None, None),
        P("sec", None),
        P("sec", None, None),
        P("sec", None, None),
        P("sec", None, None),
        P("sec", None, None),
    )
    return jax.shard_map(
        functools.partial(local, mesh.shape["sec"], mesh.shape["img"]),
        mesh=mesh,
        in_specs=placed,
        out_specs=(
            P("sec", None, "img", None, None, None),
            P("sec", "img", None),
            P("sec", "img", None),
            P("sec", "img", None),
            P("sec", "img", None),
        ),
        check_vma=False,
    )
```

```python
import functools

import jax
import jax.numpy as jnp
import numpy as np
from jax import lax
from jax.experimental import pallas as pl
from jax.experimental.pallas import tpu as pltpu
from jax.sharding import PartitionSpec as P

F32 = jnp.float32
BF16 = jnp.bfloat16
LANES = 128
WIDE = 256
MESH = pl.DeviceIdType.MESH
TWO = 2
CHUNKS = 3
GRANT = 40 * 2**20


def up(value, unit):
    return -(-value // unit) * unit


def turned(block, shift):
    shift = shift % block.shape[0]
    return block if shift == 0 else pltpu.roll(block, shift, 0)


def rows_at(even, odd, pair, offset, lanes):
    if offset % 2 == 0:
        block = even[pair + offset // 2 + 1, :, lanes]
    else:
        block = odd[pair + (offset + 1) // 2, :, lanes]
    return block.reshape(-1, 8, WIDE)


def rolled(even, odd, taps, kernel, pair, lanes, back):
    radius = kernel // 2
    held = [rows_at(even, odd, pair, k - radius, lanes) for k in range(kernel)]
    total = None
    for col_tap in range(kernel):
        part = None
        for row_tap in range(kernel):
            at = kernel - 1 - row_tap if back else row_tap
            term = taps[row_tap * kernel + col_tap, :, lanes][None] * held[at]
            part = term if part is None else part + term
        wide = part.astype(F32).reshape(-1, WIDE)
        moved = turned(wide, col_tap - radius if back else radius - col_tap)
        total = moved if total is None else total + moved
    return total


def filtered(even, odd, taps, kernel, group, select, parts, back):
    radius = kernel // 2
    breadth, wides = even.shape[1:]
    for slot, pair in enumerate(group):
        for first in range(0, wides, WIDE):
            lanes = slice(first, first + WIDE)
            held = [rows_at(even, odd, pair, k - radius, lanes) for k in range(kernel)]
            for col_tap in range(kernel):
                part = None
                for row_tap in range(kernel):
                    at = kernel - 1 - row_tap if back else row_tap
                    term = taps[row_tap * kernel + col_tap, :, lanes][None] * held[at]
                    part = term if part is None else part + term
                at = slot * LANES + col_tap * breadth
                parts[at : at + breadth, lanes] = part.reshape(breadth, WIDE)
    return lax.dot_general(
        select[...], parts[...], (((1,), (0,)), ((), ())), preferred_element_type=F32
    )


def selection(breadth, width, kernel, back):
    table = np.zeros((TWO * breadth, TWO * LANES), np.float32)
    for slot in range(TWO):
        for col_tap in range(kernel):
            shift = kernel // 2 - col_tap if back else col_tap - kernel // 2
            for col in range(width):
                if 0 <= col + shift < width:
                    at = slot * LANES + col_tap * breadth + col + shift
                    table[slot * breadth + col, at] = 1.0
    return jnp.asarray(table, BF16)


def tap_folds(even, odd, back, folds, kernel, pair):
    radius = kernel // 2
    breadth, wides = even.shape[1:]
    for first in range(0, wides, WIDE):
        lanes = slice(first, first + WIDE)
        held = [rows_at(even, odd, pair, k - radius, lanes) for k in range(kernel)]
        wide = back[pair + 1, :, lanes].astype(F32)
        for col_tap in range(kernel):
            other = turned(wide, col_tap - radius).astype(BF16).reshape(-1, 8, WIDE)
            for row_tap in range(kernel):
                term = held[row_tap] * other
                folded = term[0]
                for part in range(1, term.shape[0]):
                    folded = folded + term[part]
                tap = row_tap * kernel + col_tap
                folds[tap * 8 : tap * 8 + 8, lanes] = folded


def gathering(count):
    table = np.zeros((up(count, 8), up(count * 8, LANES)), np.float32)
    for tap in range(count):
        table[tap, tap * 8 : tap * 8 + 8] = 1.0
    return jnp.asarray(table, BF16)


def selection(breadth, width, kernel, back):
    table = np.zeros((TWO * breadth, TWO * LANES), np.float32)
    for slot in range(TWO):
        for col_tap in range(kernel):
            shift = kernel // 2 - col_tap if back else col_tap - kernel // 2
            for col in range(width):
                if 0 <= col + shift < width:
                    at = slot * LANES + col_tap * breadth + col + shift
                    table[slot * breadth + col, at] = 1.0
    return jnp.asarray(table, BF16)


def tap_sums(even, odd, back, sums, kernel, pair, lanes):
    radius = kernel // 2
    held = [rows_at(even, odd, pair, k - radius, lanes) for k in range(kernel)]
    wide = back[pair + 1, :, lanes].astype(F32)
    for col_tap in range(kernel):
        moved = turned(wide, col_tap - radius).astype(BF16).reshape(-1, 8, WIDE)
        for row_tap in range(kernel):
            term = held[row_tap] * moved
            folded = term[0]
            for part in range(1, term.shape[0]):
                folded = folded + term[part]
            tap = row_tap * kernel + col_tap
            sums[tap, :, lanes] = sums[tap, :, lanes] + folded.astype(F32)


def kernel_body(
    sections,
    group,
    kernels,
    spans,
    plan,
    last,
    older,
    arriving,
    head,
    depth_five,
    depth_three,
    point_five,
    point_three,
    select_five,
    select_three,
    select_five_back,
    select_three_back,
    gather_five,
    gather_three,
    outgoing,
    out_points,
    out_taps,
    inbox,
    outbox,
    final,
    even_last,
    odd_last,
    even_older,
    odd_older,
    even_five,
    odd_five,
    even_three,
    odd_three,
    mixed_five,
    mixed_three,
    parts_five,
    parts_three,
    point_both,
    folds_five,
    folds_three,
    taps_five,
    taps_three,
    total_five,
    total_three,
    sums_five,
    sums_three,
    sums_all,
    give_five,
    give_three,
    give_taps,
    take_five,
    take_three,
    take_taps,
    relay_three,
    relay_five,
    local_sem,
    send_sem,
    recv_sem,
    give_sem,
    take_sem,
    final_sem,
    weight_sem,
    raw,
    head_sem,
):
    five, three = kernels
    turns, height, width, channels = last.shape
    breadth = inbox.shape[3]
    rows = channels // group
    pairs = spans[-1][1]
    blocks = 2 * channels // WIDE
    columns = channels // LANES
    end = turns - 1
    folded = group == 4
    sec = lax.axis_index("sec")
    img = lax.axis_index("img")
    top = sec == sections - 1
    bottom = sec == 0
    not_top = sec < sections - 1
    not_bottom = sec > 0

    def lines(span):
        return 2 * span[0], min(2 * span[1], height)

    def first_copy(which):
        target = inbox.at[0, which, pl.ds(0, height)]
        return pltpu.make_async_copy(arriving.at[which], target, local_sem.at[which])

    def head_copy(turn):
        return pltpu.make_async_copy(head.at[turn - 1], raw.at[turn - 1], head_sem.at[turn - 1])

    @pl.when(top)
    def _():
        for turn in range(1, turns):
            head_copy(turn).start()

    def take_head(turn):
        edge = jnp.zeros((breadth - width, channels), F32)
        head_copy(turn).wait()

        def one(row, carry):
            both = raw[turn - 1, row].astype(F32)
            for which in range(2):
                own = both[:, which]
                inbox[turn, which, row] = jnp.concatenate([own, edge], 0).astype(BF16)
            return carry

        lax.fori_loop(0, height, one, 0, unroll=3)

    weights = [
        pltpu.make_async_copy(
            source, point_both.at[pl.ds(at * channels, channels)], weight_sem.at[at]
        )
        for at, source in enumerate((point_five, point_three))
    ]
    for which in range(2):
        first_copy(which).start()
        weights[which].start()

    barrier = pltpu.get_barrier_semaphore()
    for step in range(1, group):
        pl.semaphore_signal(
            barrier,
            inc=1,
            device_id={"sec": sec, "img": lax.rem(img + step, group)},
            device_id_type=MESH,
        )

    @pl.when(not_bottom)
    def _():
        pl.semaphore_signal(
            barrier, inc=1, device_id={"sec": sec - 1, "img": img}, device_id_type=MESH
        )

    @pl.when(not_top)
    def _():
        pl.semaphore_signal(
            barrier, inc=1, device_id={"sec": sec + 1, "img": img}, device_id_type=MESH
        )

    edge_even = jnp.zeros(even_five.shape[2:], BF16)

    def clear(turn, carry):
        for ref in (even_last, even_older, even_five, even_three):
            ref[turn, 0] = edge_even
            ref[turn, pairs + 1] = edge_even
        for ref in (odd_last, odd_older, odd_five, odd_three):
            ref[turn, pairs] = edge_even
        return carry

    lax.fori_loop(0, turns, clear, 0)
    for wide, packed in ((depth_five, taps_five), (depth_three, taps_three)):
        for tap in range(packed.shape[0]):
            value = jnp.broadcast_to(wide[tap : tap + 1].astype(F32), (8, channels))
            packed[tap] = jnp.concatenate([value, value], 1).astype(BF16)

    def prepare(turn):
        slot = plan[0, turn]
        zeros = jnp.zeros((breadth, channels), BF16)
        edge = jnp.zeros((breadth - width, channels), F32)
        for saved, even, odd in ((last, even_last, odd_last), (older, even_older, odd_older)):
            for row in range(-1, 2 * pairs):
                inside = 0 <= row < height
                active = zeros
                if inside:
                    raised = jnp.maximum(saved[slot, row], 0).astype(F32)
                    active = jnp.concatenate([raised, edge], 0).astype(BF16)
                lanes = slice((row % 2) * channels, (row % 2 + 1) * channels)
                if row >= 0:
                    even[turn, row // 2 + 1, :, lanes] = active
                if row < 2 * pairs - 1:
                    lanes = slice((1 - row % 2) * channels, (2 - row % 2) * channels)
                    odd[turn, (row + 1) // 2, :, lanes] = active

    def hop(turn, which, part):
        start, stop = lines(spans[part])
        return pltpu.make_async_remote_copy(
            src_ref=outbox.at[turn, which, pl.ds(start, stop - start)],
            dst_ref=inbox.at[turn + 1, which, pl.ds(start, stop - start)],
            send_sem=send_sem.at[turn, which, part],
            recv_sem=recv_sem.at[turn, which, part],
            device_id={"sec": lax.max(sec - 1, 0), "img": img},
            device_id_type=MESH,
        )

    def arrive(turn, which, part):
        if which == 0 and part == 0:

            @pl.when(jnp.logical_and(turn > 0, top))
            def _():
                take_head(turn)

        @pl.when(jnp.logical_and(turn > 0, not_top))
        def _():
            hop(turn - 1, which, part).wait_recv()

    def pull(turn):
        grad = inbox[turn, 0, 0:height].reshape(-1, channels)
        product = lax.dot_general(
            grad, point_both[...], (((1,), (1,)), ((), ())), preferred_element_type=F32
        )
        for even, odd, first in (
            (even_five, odd_five, 0),
            (even_three, odd_three, channels),
        ):

            def line(row):
                if 0 <= row < height:
                    at = row * breadth
                    return product[at : at + breadth, first : first + channels].astype(BF16)
                return jnp.zeros((breadth, channels), BF16)

            for pair in range(pairs):
                for side in range(2):
                    lanes = slice(side * channels, (side + 1) * channels)
                    even[turn, pair + 1, :, lanes] = line(2 * pair + side)
                    odd[turn, pair, :, lanes] = line(2 * pair - 1 + side)

    def parts(pair, block):
        for part in range(WIDE // LANES):
            at = block * (WIDE // LANES) + part
            lanes = slice((at % columns) * LANES, (at % columns + 1) * LANES)
            yield 2 * pair + at // columns, lanes, slice(part * LANES, (part + 1) * LANES)

    def each_block(work, span):
        def one(pair, carry):
            for block in range(blocks):
                work(pair, block, slice(block * WIDE, (block + 1) * WIDE))
            return carry

        lax.fori_loop(span[0], span[1], one, 0)

    def compact_five(turn, target, span):
        wide_to = target.shape[1]

        def work(pair, block, wide):
            out = rolled(
                even_five.at[turn], odd_five.at[turn], taps_five, five, pair, wide, True
            )
            kept = jnp.where(even_last[turn, pair + 1, :, wide].astype(F32) > 0, out, 0.0)
            for at, lanes, cut in parts(pair, block):
                own = inbox[turn, 0, at, :, lanes].astype(F32)
                extra = inbox[turn, 1, at, :, lanes].astype(F32)
                done = kept[:, cut] + own + extra
                target[at, :, lanes] = done[0:wide_to].astype(BF16)

        each_block(work, span)

    def compact_three(turn, target, span):
        wide_to = target.shape[1]

        def work(pair, block, wide):
            out = rolled(
                even_three.at[turn], odd_three.at[turn], taps_three, three, pair, wide, True
            )
            kept = jnp.where(even_older[turn, pair + 1, :, wide].astype(F32) > 0, out, 0.0)
            for at, lanes, cut in parts(pair, block):
                target[at, :, lanes] = kept[0:wide_to, cut].astype(BF16)

        each_block(work, span)

    def groups(span):
        for count, first in enumerate(range(span[0], span[1], TWO)):
            yield count % 2, range(first, min(first + TWO, span[1]))

    def sides(group, out):
        for slot, pair in enumerate(group):
            for side in range(2):
                lanes = slice(side * channels, (side + 1) * channels)
                at = slot * breadth
                yield pair, 2 * pair + side, lanes, out[at : at + breadth, lanes]

    def through_five(turn, target, span):
        wide_to = target.shape[1]
        for odds, group in groups(span):
            out = filtered(
                even_five.at[turn],
                odd_five.at[turn],
                taps_five,
                five,
                group,
                select_five_back,
                parts_five.at[odds],
                True,
            )
            for pair, row, lanes, value in sides(group, out):
                kept = jnp.where(even_last[turn, pair + 1, :, lanes].astype(F32) > 0, value, 0.0)
                own = inbox[turn, 0, row].astype(F32)
                extra = inbox[turn, 1, row].astype(F32)
                target[row] = (kept + own + extra)[0:wide_to].astype(BF16)

    def through_three(turn, target, span):
        wide_to = target.shape[1]
        for odds, group in groups(span):
            out = filtered(
                even_three.at[turn],
                odd_three.at[turn],
                taps_three,
                three,
                group,
                select_three_back,
                parts_three.at[odds],
                True,
            )
            for pair, row, lanes, value in sides(group, out):
                kept = jnp.where(even_older[turn, pair + 1, :, lanes].astype(F32) > 0, value, 0.0)
                target[row] = kept[0:wide_to].astype(BF16)

    def forward(turn, span):
        for odds, group in groups(span):
            for even, odd, taps, mixed, kernel, select, held in (
                (even_last, odd_last, taps_five, mixed_five, five, select_five, parts_five),
                (even_older, odd_older, taps_three, mixed_three, three, select_three, parts_three),
            ):
                out = filtered(
                    even.at[turn], odd.at[turn], taps, kernel, group, select, held.at[odds], False
                )
                for pair, row, lanes, value in sides(group, out):
                    mixed[lax.rem(turn, 2), row] = value.astype(BF16)

    def add_taps(turn):
        for pair in range(pairs):
            for even, odd, back, folds, gathers, sums, kernel in (
                (even_last, odd_last, even_five, folds_five, gather_five, sums_five, five),
                (even_older, odd_older, even_three, folds_three, gather_three, sums_three, three),
            ):
                held = folds.at[pair % 2]
                tap_folds(even.at[turn], odd.at[turn], back.at[turn], held, kernel, pair)
                sums[...] += jnp.dot(gathers[...], held[...], preferred_element_type=F32)

    def add_point(turn, mixed, total):
        flat = mixed[0:height].reshape(-1, channels)
        grad = inbox[turn, 0, 0:height].reshape(-1, channels)
        total[...] += lax.dot_general(
            flat, grad, (((0,), (0,)), ((), ())), preferred_element_type=F32
        )

    def share(part, step):
        source = (give_three, give_five, give_taps)[part]
        target = (take_three, take_five, take_taps)[part]
        peer = lax.rem(img + step, group)
        return pltpu.make_async_remote_copy(
            src_ref=source.at[peer],
            dst_ref=target.at[step],
            send_sem=give_sem.at[part, step],
            recv_sem=take_sem.at[part, step],
            device_id={"sec": sec, "img": peer},
            device_id_type=MESH,
        )

    pieces = range(len(spans))

    def send(turn, which, part):
        @pl.when(not_bottom)
        def _():
            hop(turn, which, part).start()

    def chain_five(turn):
        for part in pieces:
            arrive(turn, 1, part)
            through_five(turn, outbox.at[turn, 0], spans[part])
            send(turn, 0, part)

    def chain_three(turn):
        for part in pieces:
            through_three(turn, outbox.at[turn, 1], spans[part])
            send(turn, 1, part)

    def add_points(turn):
        held = lax.rem(turn, 2)
        add_point(turn, mixed_three.at[held], total_three)
        add_point(turn, mixed_five.at[held], total_five)

    def finish_points():
        for part in pieces:
            arrive(end, 0, part)
        for part, mixed, total, give in (
            (0, mixed_three, total_three, give_three),
            (1, mixed_five, total_five, give_five),
        ):
            add_point(end, mixed.at[end % 2], total)
            for peer in range(group):
                give[peer] = total[peer * rows : (peer + 1) * rows].astype(BF16)
            start_share(part)

        if folded:

            @pl.when(outer)
            def _():
                pass_on(0, give_three.at[mate], 2, 2, mate).start()
                pass_on(1, give_five.at[mate], 2, 2, mate).start()

    side = img // 2
    mate = img + 1 - 2 * (img % 2)
    far_inner, far_outer = 2 - side, 3 - 3 * side
    inner = (img + 1) // 2 % 2 == 1
    outer = (img + 1) // 2 % 2 == 0

    def pass_on(part, source, slot, sender, peer):
        target = (take_three, take_five)[part]
        return pltpu.make_async_remote_copy(
            src_ref=source,
            dst_ref=target.at[slot],
            send_sem=give_sem.at[part, sender],
            recv_sem=take_sem.at[part, slot],
            device_id={"sec": sec, "img": peer},
            device_id_type=MESH,
        )

    def start_share(part):
        give = (give_three, give_five)[part]
        if not folded:
            for step in range(1, group):
                share(part, step).start()
            return

        @pl.when(outer)
        def _():
            pass_on(part, give.at[far_outer], 0, 0, mate).start()
            pass_on(part, give.at[far_inner], 1, 1, mate).start()

        @pl.when(inner)
        def _():
            pass_on(part, give.at[mate], 2, 2, mate).start()

    def relay(part):
        if not folded:
            return
        give, take = ((give_three, take_three), (give_five, take_five))[part]
        held = (relay_three, relay_five)[part]

        @pl.when(inner)
        def _():
            for slot, peer in ((0, far_outer), (1, far_inner)):
                pass_on(part, give.at[peer], slot, slot, mate).wait_recv()
                held[slot] = (give[peer].astype(F32) + take[slot].astype(F32)).astype(BF16)
                pass_on(part, held.at[slot], 3, slot, peer).start()

    prepare(0)
    for ref in (parts_five, parts_three):
        ref[...] = jnp.zeros(ref.shape, ref.dtype)
    callers = group + 1 - bottom.astype(jnp.int32) - top.astype(jnp.int32)
    for which in range(2):
        first_copy(which).wait()
        weights[which].wait()
    pull(0)
    pl.semaphore_wait(barrier, callers)

    def turn_work(turn, carry):
        @pl.when(turn > 0)
        def _():
            for part in pieces:
                arrive(turn, 0, part)
            pull(turn)

        chain_five(turn)
        chain_three(turn)

        @pl.when(turn == 0)
        def _():
            for ref in (
                folds_five,
                folds_three,
                sums_five,
                sums_three,
                total_five,
                total_three,
                sums_all,
            ):
                ref[...] = jnp.zeros(ref.shape, ref.dtype)

        prepare(turn + 1)

        def ahead(later, carry):
            forward(later, (0, pairs))
            return carry

        lax.fori_loop(turn + lax.min(turn, 1), turn + 2, ahead, 0)
        add_points(turn)
        return carry

    lax.fori_loop(0, end, turn_work, 0)
    finish_points()
    pull(end)

    def all_taps(turn, carry):
        @pl.when(turn == turns // 2)
        def _():
            relay(0)

        add_taps(turn)
        return carry

    lax.fori_loop(0, turns, all_taps, 0)
    relay(1)
    count_five, count_three = five * five, three * three
    for sums, start, count in ((sums_five, 0, count_five), (sums_three, count_five, count_three)):
        sums_all[start : start + count] = sums[0:count, 0:channels] + sums[0:count, channels:]
    flipped = sums_all[...].T
    for peer in range(group):
        own = flipped[peer * rows : (peer + 1) * rows].T
        give_taps[peer] = own[0 : give_taps.shape[1]].astype(BF16)
    for step in range(1, group):
        share(2, step).start()
    for part in range(len(spans)):
        arrive(end, 1, part)
    compact_five(end, final.at[0], (0, pairs))
    compact_three(end, final.at[1], (0, pairs))
    finals = [
        pltpu.make_async_copy(
            final.at[which, pl.ds(0, height)], outgoing.at[which], final_sem.at[which]
        )
        for which in range(2)
    ]
    for copy in finals:
        copy.start()

    def gathered(part, give, take):
        value = give[img].astype(F32)
        if folded and part < 2:
            for slot in (2, 3):
                pass_on(part, give.at[mate], slot, 2, mate).wait_recv()
                value = value + take[slot].astype(F32)
            return value
        for step in range(1, group):
            share(part, step).wait_recv()
            value = value + take[step].astype(F32)
        return value

    out_points[1] = gathered(0, give_three, take_three)
    out_points[0] = gathered(1, give_five, take_five)
    by_tap = gathered(2, give_taps, take_taps)
    for tap in range(count_five + count_three):
        out_taps[tap] = by_tap[tap : tap + 1]
    for part in range(3):
        for step in range(1, group):
            if folded and part < 2:
                source = (give_three, give_five)[part].at[mate]
                pass_on(part, source, 2, step - 1, mate).wait_send()
            else:
                share(part, step).wait_send()
    for copy in finals:
        copy.wait()

    @pl.when(not_bottom)
    def _():
        for turn in range(end):
            for which in range(2):
                for part in range(len(spans)):
                    hop(turn, which, part).wait_send()


def scale_body(factor, points, taps, five, three, taps_five, taps_three):
    count = taps_five.shape[0]
    five[...] = points[0] * factor
    three[...] = points[1] * factor
    taps_five[...] = taps[0:count] * factor
    taps_three[...] = taps[count:] * factor


def local(
    sections,
    group,
    saved_last,
    saved_older,
    arriving,
    head_adjoint,
    plan,
    depth_five,
    depth_three,
    point_five,
    point_three,
):
    turns, _, height, width, channels = saved_last.shape[1:]
    count_five, count_three = depth_five.shape[1], depth_three.shape[1]
    five, three = round(count_five**0.5), round(count_three**0.5)
    breadth = up(width + five // 2, 8)
    pairs = up(height, 2) // 2
    even = pltpu.VMEM((turns, pairs + 2, breadth, 2 * channels), BF16)
    odd = pltpu.VMEM((turns, pairs + 1, breadth, 2 * channels), BF16)
    rows = channels // group
    factor = 1.0 / (height * width)
    chunk = -(-pairs // CHUNKS)
    spans = tuple((at, min(at + chunk, pairs)) for at in range(0, pairs, chunk))
    vmem = pl.BlockSpec(memory_space=pltpu.VMEM)
    smem = pl.BlockSpec(memory_space=pltpu.SMEM)
    outside = pl.BlockSpec(memory_space=pl.ANY)
    fixed = pl.BlockSpec(memory_space=pltpu.HBM)
    in_hbm = functools.partial(
        pltpu.with_memory_space_constraint, memory_space=pltpu.HBM
    )
    body = functools.partial(kernel_body, sections, group, (five, three), spans)
    grow = (0, breadth - width)
    outgoing, points, taps = pl.pallas_call(
        body,
        out_shape=(
            jax.ShapeDtypeStruct((2, height, width, channels), BF16),
            jax.ShapeDtypeStruct((2, rows, channels), F32),
            jax.ShapeDtypeStruct((count_five + count_three, 1, rows), F32),
        ),
        in_specs=[smem, vmem, vmem, outside, fixed, *[vmem] * 2, *[fixed] * 2, *[vmem] * 6],
        out_specs=(outside, *[vmem] * 2),
        scratch_shapes=[
            pltpu.VMEM((turns, 2, 2 * pairs, breadth, channels), BF16),
            pltpu.VMEM((turns - 1, 2, 2 * pairs, breadth, channels), BF16),
            pltpu.VMEM((2, 2 * pairs, width, channels), BF16),
            *([even, odd] * 4),
            pltpu.VMEM((2, 2 * pairs, breadth, channels), BF16),
            pltpu.VMEM((2, 2 * pairs, breadth, channels), BF16),
            pltpu.VMEM((2, TWO * LANES, 2 * channels), BF16),
            pltpu.VMEM((2, TWO * LANES, 2 * channels), BF16),
            pltpu.VMEM((2 * channels, channels), BF16),
            pltpu.VMEM((2, up(count_five * 8, LANES), 2 * channels), BF16),
            pltpu.VMEM((2, up(count_three * 8, LANES), 2 * channels), BF16),
            pltpu.VMEM((count_five, 8, 2 * channels), BF16),
            pltpu.VMEM((count_three, 8, 2 * channels), BF16),
            pltpu.VMEM((channels, channels), F32),
            pltpu.VMEM((channels, channels), F32),
            pltpu.VMEM((up(count_five, 8), 2 * channels), F32),
            pltpu.VMEM((up(count_three, 8), 2 * channels), F32),
            pltpu.VMEM((LANES, channels), F32),
            pltpu.VMEM((group, rows, channels), BF16),
            pltpu.VMEM((group, rows, channels), BF16),
            pltpu.VMEM((group, up(count_five + count_three, 16), rows), BF16),
            pltpu.VMEM((group, rows, channels), BF16),
            pltpu.VMEM((group, rows, channels), BF16),
            pltpu.VMEM((group, up(count_five + count_three, 16), rows), BF16),
            pltpu.VMEM((2, rows, channels), BF16),
            pltpu.VMEM((2, rows, channels), BF16),
            pltpu.SemaphoreType.DMA((2,)),
            pltpu.SemaphoreType.DMA((turns - 1, 2, len(spans))),
            pltpu.SemaphoreType.DMA((turns - 1, 2, len(spans))),
            pltpu.SemaphoreType.DMA((3, group)),
            pltpu.SemaphoreType.DMA((3, group)),
            pltpu.SemaphoreType.DMA((2,)),
            pltpu.SemaphoreType.DMA((2,)),
            pltpu.VMEM((turns - 1, height, width, 2, channels), BF16),
            pltpu.SemaphoreType.DMA((turns - 1,)),
        ],
        compiler_params=pltpu.CompilerParams(
            collective_id=0, has_side_effects=True, vmem_limit_bytes=GRANT
        ),
    )(
        plan,
        saved_last.reshape(turns, height, width, channels),
        saved_older.reshape(turns, height, width, channels),
        jnp.pad(arriving[0, :, 0], ((0, 0), (0, 0), grow, (0, 0))),
        in_hbm(head_adjoint[:, :, 0].transpose(0, 2, 3, 1, 4)),
        depth_five[0],
        depth_three[0],
        in_hbm(point_five[0]),
        in_hbm(point_three[0]),
        *(
            selection(breadth, width, kernel, back)
            for back in (False, True)
            for kernel in (five, three)
        ),
        *(gathering(count) for count in (count_five, count_three)),
    )
    grad_five, grad_three, taps_five, taps_three = pl.pallas_call(
        functools.partial(scale_body, factor),
        out_shape=(
            jax.ShapeDtypeStruct((rows, channels), F32),
            jax.ShapeDtypeStruct((rows, channels), F32),
            jax.ShapeDtypeStruct((count_five, 1, rows), F32),
            jax.ShapeDtypeStruct((count_three, 1, rows), F32),
        ),
        in_specs=[vmem, vmem],
        out_specs=(vmem,) * 4,
        compiler_params=pltpu.CompilerParams(vmem_limit_bytes=GRANT),
    )(points, taps)
    return (
        outgoing.reshape(1, 2, 1, height, width, channels),
        grad_five[None],
        taps_five.transpose(1, 2, 0),
        grad_three[None],
        taps_three.transpose(1, 2, 0),
    )


def solution(mesh):
    placed = (
        P("sec", None, "img", None, None, None),
        P("sec", None, "img", None, None, None),
        P("sec", None, "img", None, None, None),
        P(None, None, "img", None, None, None),
        P("sec", None),
        P("sec", None, None),
        P("sec", None, None),
        P("sec", None, None),
        P("sec", None, None),
    )
    return jax.shard_map(
        functools.partial(local, mesh.shape["sec"], mesh.shape["img"]),
        mesh=mesh,
        in_specs=placed,
        out_specs=(
            P("sec", None, "img", None, None, None),
            P("sec", "img", None),
            P("sec", "img", None),
            P("sec", "img", None),
            P("sec", "img", None),
        ),
        check_vma=False,
    )
```
